512 devices in a mesh: box: 128 (over z, y, core), field: 4 (over x).
Axes of the slice: x: 4, y: 8, z: 8, core: 2. Of those that a mesh axis runs over, the one named last changes fastest.
Arguments:
- incident: bfloat16 [2, 2048, 65536], P(None, 'field', 'box'), may hold values from -6 to 6
- leaf_inverse: bfloat16 [128, 2, 512, 512], P('box', None, 'field'), may hold values from -0.1875 to 0.1875
- contrast: float32 [65536], P('box'), may hold values from 0.2 to 1
- skel_index: int32 [128, 2, 256], replicated, may hold values from 0 to 511
- ranks: int32 [128, 2], replicated, may hold values from 128 to 256, as said below
- top_core: bfloat16 [2, 256, 8192], P(None, None, 'box'), may hold values from -0.25 to 0.25
Outputs:
- total_field: float32 [2, 2048, 65536], P(None, 'field', 'box')
The draws below stay inside these ranges and needn't reach their ends.
Inputs may be any that keep to these rules, and one draw needn't show every extreme that they name: At each level some box has rank exactly 256; most ranks lie near 256 // 2.
All inputs are finite; a program needn't handle non-finite values.
Results may differ from the reference program's by a relative error of at most 0.0003.
Values may be sent and summed in bfloat16 or wider, within the bound.
A program may use at most 64 MiB of HBM per device.

```python
import math
import jax
import jax.numpy as jnp
from jax import lax

SIDE = 8
LEAF = 512
KMAX = 256
KQ = 64
NF = 2048
BOXES = 128
POINTS = 65536


def draw_ranks(key, part):
    key_a, key_b, key_c = jax.random.split(key, 3)
    spread = KMAX - KMAX // 2
    first = jax.random.randint(key_a, (BOXES, 2), 0, spread + 1)
    second = jax.random.randint(key_b, (BOXES, 2), 0, spread + 1)
    drawn = KMAX // 2 + first * second // spread
    chosen = jax.random.randint(key_c, (2,), 0, BOXES)
    drawn = drawn.at[chosen, jnp.arange(2)].set(KMAX)
    return drawn.astype(jnp.int32)


def touch_ends(values, rng, smallest, largest):
    shape = values.shape
    place = [jax.random.randint(jax.random.fold_in(rng, axis), (), 0, shape[axis]) for axis in range(len(shape))]
    values = values.at[tuple(place)].set(smallest)
    longest = shape.index(max(shape))
    place[longest] = (place[longest] + 1) % shape[longest]
    return values.at[tuple(place)].set(largest)


def block_scale(rng, dims, shards, least, high):
    gain = 1.0
    for axis_at, shards_of in shards:
        heights = jax.random.uniform(jax.random.fold_in(jax.random.fold_in(rng, 6), axis_at), (shards_of,), jnp.float32, least / len(shards), high / len(shards))
        gain = gain * jnp.repeat(jnp.exp(heights), dims[axis_at] // shards_of).reshape((-1,) + (1,) * (len(dims) - 1 - axis_at))
    return gain


def bell_draw(rng, dims, scale, most, shards=(), held_as=jnp.bfloat16):
    array = jax.random.normal(rng, dims, jnp.float32) * scale
    if len(shards) > 0:
        array = block_scale(rng, dims, shards, -0.22, 0.18) * array
    return jnp.clip(array, min=-most, max=most).astype(held_as)


def setup_inputs(seed: int = 0) -> dict:
    key_list = jax.random.split(jax.random.key(seed), 7)
    incident = bell_draw(key_list[0], (2, NF, POINTS), 1.0, 6.0, ((1, 4), (2, 128)))
    leaf_inverse = bell_draw(key_list[1], (BOXES, 2, LEAF, LEAF), (2 * LEAF) ** -0.5, 0.1875, ((0, 128), (2, 4)))
    contrast = jnp.clip(jnp.exp(math.log(1.0) - 1.609438 * jax.random.uniform(key_list[2], (POINTS,), jnp.float32) ** block_scale(key_list[2], (POINTS,), ((0, 128),), -0.2, 0.2)), 0.2, 1.0)
    skel_index = touch_ends(jax.random.randint(key_list[3], (BOXES, 2, KMAX), 0, LEAF), jax.random.fold_in(key_list[3], 1), 0, LEAF - 1).astype(jnp.int32)
    ranks = draw_ranks(jax.random.fold_in(key_list[6], 71), 0)
    top_core = bell_draw(key_list[5], (2, KMAX, BOXES * KQ), (2 * KMAX) ** -0.5, 0.25, ((2, 128),))
    return {"incident": incident, "leaf_inverse": leaf_inverse, "contrast": contrast, "skel_index": skel_index, "ranks": ranks, "top_core": top_core}


WAVENUM = 0.7
HIGH = lax.Precision.HIGHEST

def positions(box_at, index_list):
    px = (SIDE * box_at + index_list % SIDE).astype(jnp.float32)
    py = (index_list // SIDE % SIDE).astype(jnp.float32)
    pz = (index_list // (SIDE * SIDE)).astype(jnp.float32)
    return jnp.stack([px, py, pz])

def selector(index_list, rank_now):
    rows = jnp.arange(KMAX, dtype=jnp.int32)[:, None]
    cols = jnp.arange(LEAF, dtype=jnp.int32)[None, :]
    hit = (index_list[:, None] == cols) & (rows < rank_now)
    return hit.astype(jnp.float32)

def kernel_parts(own_pos, far_pos):
    diff = own_pos[:, :, None] - far_pos[:, None, :]
    dist = jnp.sqrt(lax.optimization_barrier(jnp.sum(diff * diff, axis=0)))
    return (jnp.cos(WAVENUM * dist) / dist, jnp.sin(WAVENUM * dist) / dist)

def complex_apply(mat_re, mat_im, vec):
    out_re = jnp.einsum('km,fm->fk', mat_re, vec[0], precision=HIGH) - jnp.einsum('km,fm->fk', mat_im, vec[1], precision=HIGH)
    out_im = jnp.einsum('km,fm->fk', mat_re, vec[1], precision=HIGH) + jnp.einsum('km,fm->fk', mat_im, vec[0], precision=HIGH)
    return jnp.stack([out_re, out_im])

def reference(incident, leaf_inverse, contrast, skel_index, ranks, top_core):
    fields_in = incident.astype(jnp.float32).reshape(2, NF, BOXES, LEAF).transpose(2, 0, 1, 3)

    def leaf_solve(pair):
        mat, vec = pair
        mat = mat.astype(jnp.float32)
        return complex_apply(mat[0], mat[1], vec)
    state = lax.map(leaf_solve, (leaf_inverse, fields_in))
    weights_c = contrast.reshape(BOXES, LEAF)
    box_ids = jnp.arange(BOXES, dtype=jnp.int32)
    for merge_level in range(2):

        def weighted(pair):
            field_b, idx_b, rank_b, cont_b = pair
            sel = selector(idx_b, rank_b)
            skel_vals = jnp.einsum('cfn,kn->cfk', field_b, sel, precision=HIGH)
            skel_q = jnp.dot(sel, cont_b, precision=HIGH)
            return skel_vals * skel_q
        sent = lax.map(weighted, (state, skel_index[:, merge_level], ranks[:, merge_level], weights_c))
        partners = jnp.bitwise_xor(box_ids, 1 << merge_level)
        received = sent[partners]

        def couple(pair):
            field_b, box_at, far_at, far_vals = pair
            idx_b = skel_index[box_at, merge_level]
            idx_p = skel_index[far_at, merge_level]
            sel = selector(idx_b, ranks[box_at, merge_level])
            green_re, green_im = kernel_parts(positions(box_at, idx_b), positions(far_at, idx_p))
            pushed = complex_apply(green_re, green_im, far_vals)
            return field_b - jnp.einsum('cfk,kn->cfn', pushed, sel, precision=HIGH)
        state = lax.map(couple, (state, box_ids, partners, received))
    cores = top_core.astype(jnp.float32).reshape(2, KMAX, BOXES // 4, KMAX)

    def apply_core(pair):
        field_b, box_at = pair
        sel = selector(skel_index[box_at, 1], ranks[box_at, 1])
        coarse = jnp.einsum('cfn,kn->cfk', field_b, sel, precision=HIGH)
        core_q = lax.dynamic_index_in_dim(cores, box_at // 4, 2, keepdims=False)
        pushed = complex_apply(core_q[0], core_q[1], coarse)
        return field_b - jnp.einsum('cfk,kn->cfn', pushed, sel, precision=HIGH)
    state = lax.map(apply_core, (state, box_ids))
    return state.transpose(1, 2, 0, 3).reshape(2, NF, POINTS)
```

```python
import functools

import jax
import jax.numpy as jnp
from jax import lax
from jax.experimental import pallas as pl
from jax.experimental.pallas import tpu as pltpu
from jax.sharding import PartitionSpec as P

MESH = pl.DeviceIdType.MESH
WAVENUM = 0.7
F32 = jnp.float32
BF16 = jnp.bfloat16
CHUNK = 128
TOP = 32767.0


def dot_nn(lhs, rhs):
    return lax.dot_general(lhs, rhs, (((1,), (0,)), ((), ())), preferred_element_type=F32)


def dot_nt(lhs, rhs):
    return lax.dot_general(lhs, rhs, (((1,), (1,)), ((), ())), preferred_element_type=F32)


def halves(value):
    high = value.astype(BF16)
    low = (value - high.astype(F32)).astype(BF16)
    return high, low


def grid_of(index):
    return index & 7, (index >> 3) & 7, index >> 6


def green(far_col, own_row, apart):
    fx, fy, fz = grid_of(far_col)
    ox, oy, oz = grid_of(own_row)
    dx = (fx - ox + apart).astype(F32)
    dy = (fy - oy).astype(F32)
    dz = (fz - oz).astype(F32)
    dist = jnp.sqrt(dx * dx + dy * dy + dz * dz)
    turn = WAVENUM * dist
    inverse = 1.0 / dist
    return jnp.cos(turn) * inverse, jnp.sin(turn) * inverse


def put_complex(ref, re, im):
    half = re.shape[0]
    ref[:half, :half] = re
    ref[:half, half:] = im
    ref[half:, :half] = -im
    ref[half:, half:] = re


def kernel(
    inc, leaf, con, skel, rank_in, core, out,
    x, a, idx, rank, cont, cq, et, es0, es1, g0h, g0l, g1h, g1l, cc,
    ws, wr, cs, cr, ss, sr, v, held,
    lsem, xsend, xrecv, csend, crecv, wsend, wrecv, ksend, krecv, ssend, srecv,
):
    fields, leafs = inc.shape[1], inc.shape[2]
    kmax = skel.shape[2]
    rows = leaf.shape[2]
    box = lax.axis_index("box")
    me = lax.axis_index("field")
    right, left, across = (me + 1) % 4, (me + 3) % 4, (me + 2) % 4
    box1 = box + 1 - 2 * (box % 2)
    box2 = box + 2 - 4 * ((box // 2) % 2)
    box3 = box2 + 1 - 2 * (box % 2)
    quad = box % 4

    def local(src, dst, at):
        copy = pltpu.make_async_copy(src, dst, lsem.at[at])
        copy.start()
        return copy

    load_idx = [
        local(skel.at[who], idx.at[at], at) for at, who in enumerate((box, box1, box2))
    ]
    load_rank = local(rank_in, rank, 3)
    load_con = local(con, cont, 4)
    load_x = local(inc, x, 5)
    load_a = local(leaf.at[0], a.at[me], 6)
    load_c = local(core, cq.at[quad], 7)

    barrier = pltpu.get_barrier_semaphore()
    for peer in ((box, right), (box, left), (box1, me), (box2, me), (box3, me)):
        pl.semaphore_signal(barrier, inc=1, device_id=peer, device_id_type=MESH)
    pl.semaphore_wait(barrier, 5)

    def remote(src, dst, send, recv, peer):
        copy = pltpu.make_async_remote_copy(
            src_ref=src, dst_ref=dst, send_sem=send, recv_sem=recv,
            device_id=peer, device_id_type=MESH,
        )
        copy.start()
        return copy

    def ring(src, owner, part, at, to):
        return remote(src, a.at[owner, part], xsend.at[at], xrecv.at[at], (box, to))

    from_left_re = ring(leaf.at[0, 0], me, 0, 0, right)
    from_right_im = ring(leaf.at[0, 1], me, 1, 3, left)
    from_left_im = ring(leaf.at[0, 1], me, 1, 1, right)
    from_right_re = ring(leaf.at[0, 0], me, 0, 4, left)
    cores = [
        remote(core, cq.at[quad], csend.at[at], crecv.at[at], (who, me))
        for at, who in enumerate((box1, box2, box3))
    ]

    for copy in load_idx:
        copy.wait()
    load_rank.wait()
    load_con.wait()
    own = idx[0]
    own0, own1 = own[0:1], own[1:2]
    far0, far1 = idx[1][0:1], idx[2][1:2]
    at_box = lax.broadcasted_iota(jnp.int32, rank.shape, 1) == box
    ranks = jnp.sum(jnp.where(at_box, rank[...].astype(F32), 0.0), axis=1, keepdims=True)
    at_k = lax.broadcasted_iota(jnp.int32, (1, kmax), 1)
    in0 = at_k.astype(F32) < ranks[0:1]
    in1 = at_k.astype(F32) < ranks[1:2]
    pick0 = jnp.where(in0, own0, -1)
    pick1 = jnp.where(in1, own1, -1)
    pick1_too = jnp.where(in1, own1, -2)
    table = jnp.concatenate([pick0, pick1, far0, far1, own0, own0, own0, own0], axis=0)
    columns = jnp.transpose(table.astype(F32)).astype(jnp.int32)

    both = jnp.concatenate([pick0, pick1], axis=1)
    at_n = lax.broadcasted_iota(jnp.int32, (rows, 2 * kmax), 0)
    contrast = cont[...]
    c_high = contrast.astype(BF16).astype(F32)
    c_mid = (contrast - c_high).astype(BF16).astype(F32)
    c_low = contrast - c_high - c_mid
    zero = jnp.zeros((5, leafs), F32)
    c_rows = jnp.concatenate([c_high, c_mid, c_low, zero], axis=0).astype(BF16)
    weight = jnp.zeros((8, 2 * kmax), F32)
    for block in range(leafs // rows):
        hit = jnp.where(at_n + block * rows == both, 1.0, 0.0).astype(BF16)
        et[block, :rows] = hit
        et[block, rows:] = hit
        weight = weight + dot_nn(c_rows[:, block * rows : (block + 1) * rows], hit)
    weight = jnp.sum(weight, axis=0, keepdims=True)
    q0, q1 = weight[:, :kmax], weight[:, kmax:]

    def block_of(owner, start, size, first):
        matrix = a[owner].reshape(2 * rows, leafs)
        at_f = pl.ds(start, size)
        by_re = dot_nt(x[0, at_f, :], matrix)
        by_im = dot_nt(x[1, at_f, :], matrix)
        y_re = by_re[:, :rows] - by_im[:, rows:]
        y_im = by_re[:, rows:] + by_im[:, :rows]
        at_cols = pl.ds(pl.multiple_of(owner * rows, rows), rows)
        out[0, at_f, at_cols] = y_re
        out[1, at_f, at_cols] = y_im
        high, low = halves(jnp.concatenate([y_re, y_im], axis=0))
        picked = dot_nn(jnp.concatenate([high, low], axis=1), et[owner])
        if not first:
            picked = picked + jnp.concatenate([v[0, at_f, :], v[1, at_f, :]], axis=0)
        v[0, at_f, :] = picked[:size]
        v[1, at_f, :] = picked[size:]

    def whole_block(owner, first):
        for start in range(0, fields, 2 * CHUNK):
            block_of(owner, start, 2 * CHUNK, first)

    load_x.wait()
    load_a.wait()
    whole_block(me, True)

    g_re, g_im = green(columns[:, 2:3], own0, 8 * (box1 - box))
    re_h, re_l = halves(g_re)
    im_h, im_l = halves(g_im)
    put_complex(g0h, re_h, im_h)
    put_complex(g0l, re_l, im_l)

    from_left_re.wait_recv()
    on_right = ring(a.at[left, 0], left, 0, 2, right)
    from_right_im.wait_recv()
    on_left = ring(a.at[right, 1], right, 1, 5, left)

    at_l = lax.broadcasted_iota(jnp.int32, (1, leafs), 1)
    lanes = jnp.concatenate([at_l, pick1_too], axis=1)
    es0[...] = jnp.where(columns[:, 0:1] == lanes, 1.0, 0.0).astype(BF16)
    es1[...] = jnp.where(columns[:, 1:2] == lanes, 1.0, 0.0).astype(BF16)

    from_left_im.wait_recv()
    whole_block(left, False)
    from_right_re.wait_recv()
    whole_block(right, False)

    g_re, g_im = green(columns[:, 3:4], own1, 8 * (box2 - box))
    re_h, re_l = halves(g_re)
    im_h, im_l = halves(g_im)
    put_complex(g1h, re_h, im_h)
    put_complex(g1l, re_l, im_l)

    load_c.wait()
    for copy in cores:
        copy.wait_recv()
    c_re = jnp.concatenate([cq[at, 0] for at in range(4)], axis=0)
    c_im = jnp.concatenate([cq[at, 1] for at in range(4)], axis=0)
    put_complex(cc, c_re, c_im)

    def first_stage(c):
        start = c * CHUNK
        at_f = pl.ds(start, CHUNK)
        block_of(across, start, CHUNK, False)
        value = jnp.concatenate([v[0, at_f, :kmax] * q0, v[1, at_f, :kmax] * q0], axis=1)
        ws[c, 0], ws[c, 1] = halves(value)
        return remote(ws.at[c], wr.at[c], wsend.at[c], wrecv.at[c], (box1, me))

    def coupled(high, low, ref_h, ref_l):
        main = dot_nn(jnp.concatenate([high, low], axis=0), ref_h[...])
        return main[:CHUNK] + main[CHUNK:] + dot_nn(high, ref_l[...])

    def spread(value, ref):
        high, low = halves(jnp.concatenate([value[:, :kmax], value[:, kmax:]], axis=0))
        both_parts = dot_nn(jnp.concatenate([high, low], axis=0), ref)
        return both_parts[: 2 * CHUNK] + both_parts[2 * CHUNK :]

    def second_stage(c, arriving):
        at_f = pl.ds(c * CHUNK, CHUNK)
        arriving.wait_recv()
        pushed = coupled(wr[c, 0], wr[c, 1], g0h, g0l)
        moved = spread(pushed, es0[...])
        v_re = v[0, at_f, kmax:] - moved[:CHUNK, leafs:]
        v_im = v[1, at_f, kmax:] - moved[CHUNK:, leafs:]
        v[0, at_f, kmax:] = v_re
        v[1, at_f, kmax:] = v_im
        most = jnp.max(jnp.maximum(jnp.abs(v_re), jnp.abs(v_im)), axis=0, keepdims=True)
        scale = TOP / jnp.maximum(most, 1e-30)
        code_re = jnp.round(v_re * scale).astype(jnp.int32).astype(jnp.int16)
        code_im = jnp.round(v_im * scale).astype(jnp.int32).astype(jnp.int16)
        cs[c, :, :kmax] = code_re
        cs[c, :, kmax:] = code_im
        step = jnp.maximum(most, 1e-30) * (1.0 / TOP) * q1
        ss[c] = jnp.broadcast_to(step, (8, kmax))
        codes = remote(cs.at[c], cr.at[c], ksend.at[c], krecv.at[c], (box2, me))
        steps = remote(ss.at[c], sr.at[c], ssend.at[c], srecv.at[c], (box2, me))
        out[0, at_f, :] = out[0, at_f, :] - moved[:CHUNK, :leafs]
        out[1, at_f, :] = out[1, at_f, :] - moved[CHUNK:, :leafs]
        return codes, steps

    def third_stage(c, codes, steps):
        at_f = pl.ds(c * CHUNK, CHUNK)
        codes.wait_recv()
        steps.wait_recv()
        step = sr[c][0:1]
        step = jnp.concatenate([step, step], axis=1)
        high, low = halves(cr[c].astype(jnp.int32).astype(F32) * step)
        pushed = coupled(high, low, g1h, g1l)
        held[...] = pushed
        again = spread(pushed, es1[:, leafs:])
        coarse = jnp.concatenate(
            [v[0, at_f, kmax:] - again[:CHUNK], v[1, at_f, kmax:] - again[CHUNK:]], axis=1
        )
        high, low = halves(coarse)
        main = dot_nn(jnp.concatenate([high, low], axis=0), cc[...])
        total = held[...] + (main[:CHUNK] + main[CHUNK:])
        moved = spread(total, es1[:, :leafs])
        out[0, at_f, :] = out[0, at_f, :] - moved[:CHUNK]
        out[1, at_f, :] = out[1, at_f, :] - moved[CHUNK:]

    on_right.wait_recv()
    on_left.wait_recv()
    chunks = fields // CHUNK
    sent = []
    codes = []
    for c in range(chunks + 1):
        if c < chunks:
            sent.append(first_stage(c))
        if c > 0:
            codes.append(second_stage(c - 1, sent[c - 1]))
    for c in range(chunks):
        third_stage(c, *codes[c])

    for copy in (from_left_re, from_left_im, from_right_im, from_right_re, on_right, on_left):
        copy.wait_send()
    for copy in cores + sent:
        copy.wait_send()
    for pair in codes:
        for copy in pair:
            copy.wait_send()


def body(incident, leaf_inverse, contrast, skel_index, ranks, top_core):
    _, fields, leafs = incident.shape
    rows = leaf_inverse.shape[2]
    kmax = skel_index.shape[2]
    boxes, kq = ranks.shape[0], top_core.shape[2]
    chunks = fields // CHUNK
    wide = 2 * kmax
    dma = pltpu.SemaphoreType.DMA
    return pl.pallas_call(
        kernel,
        out_shape=jax.ShapeDtypeStruct(incident.shape, F32),
        in_specs=[pl.BlockSpec(memory_space=pltpu.HBM)] * 6,
        out_specs=pl.BlockSpec(memory_space=pltpu.VMEM),
        scratch_shapes=[
            pltpu.VMEM((2, fields, leafs), BF16),
            pltpu.VMEM((4, 2, rows, leafs), BF16),
            pltpu.VMEM((3, 2, kmax), jnp.int32),
            pltpu.VMEM((2, boxes), jnp.int32),
            pltpu.VMEM((1, leafs), F32),
            pltpu.VMEM((4, 2, kq, kmax), BF16),
            pltpu.VMEM((4, 2 * rows, wide), BF16),
            pltpu.VMEM((kmax, leafs + kmax), BF16),
            pltpu.VMEM((kmax, leafs + kmax), BF16),
            pltpu.VMEM((wide, wide), BF16),
            pltpu.VMEM((wide, wide), BF16),
            pltpu.VMEM((wide, wide), BF16),
            pltpu.VMEM((wide, wide), BF16),
            pltpu.VMEM((wide, wide), BF16),
            pltpu.VMEM((chunks, 2, CHUNK, wide), BF16),
            pltpu.VMEM((chunks, 2, CHUNK, wide), BF16),
            pltpu.VMEM((chunks, CHUNK, wide), jnp.int16),
            pltpu.VMEM((chunks, CHUNK, wide), jnp.int16),
            pltpu.VMEM((chunks, 8, kmax), F32),
            pltpu.VMEM((chunks, 8, kmax), F32),
            pltpu.VMEM((2, fields, wide), F32),
            pltpu.VMEM((CHUNK, wide), F32),
            dma((8,)), dma((6,)), dma((6,)), dma((3,)), dma((3,)),
            dma((chunks,)), dma((chunks,)), dma((chunks,)), dma((chunks,)),
            dma((chunks,)), dma((chunks,)),
        ],
        compiler_params=pltpu.CompilerParams(
            collective_id=0, has_side_effects=True, vmem_limit_bytes=48 << 20
        ),
        name="solve",
    )(
        incident,
        leaf_inverse,
        contrast.reshape(1, leafs),
        skel_index,
        ranks.T,
        jnp.swapaxes(top_core, 1, 2),
    )


def solution(mesh):
    return jax.shard_map(
        body,
        mesh=mesh,
        in_specs=(
            P(None, "field", "box"),
            P("box", None, "field", None),
            P("box"),
            P(),
            P(),
            P(None, None, "box"),
        ),
        out_specs=P(None, "field", "box"),
        check_vma=False,
    )
```

```python
import functools

import jax
import jax.numpy as jnp
from jax import lax
from jax.experimental import pallas as pl
from jax.experimental.pallas import tpu as pltpu
from jax.sharding import PartitionSpec as P

MESH = pl.DeviceIdType.MESH
WAVENUM = 0.7
F32 = jnp.float32
BF16 = jnp.bfloat16
CHUNK = 128
TOP = 32767.0


def dot_nn(lhs, rhs):
    return lax.dot_general(lhs, rhs, (((1,), (0,)), ((), ())), preferred_element_type=F32)


def dot_nt(lhs, rhs):
    return lax.dot_general(lhs, rhs, (((1,), (1,)), ((), ())), preferred_element_type=F32)


def halves(value):
    high = value.astype(BF16)
    low = (value - high.astype(F32)).astype(BF16)
    return high, low


def grid_of(index):
    return index & 7, (index >> 3) & 7, index >> 6


def green(far_col, own_row, apart):
    fx, fy, fz = grid_of(far_col)
    ox, oy, oz = grid_of(own_row)
    dx = (fx - ox + apart).astype(F32)
    dy = (fy - oy).astype(F32)
    dz = (fz - oz).astype(F32)
    dist = jnp.sqrt(dx * dx + dy * dy + dz * dz)
    turn = WAVENUM * dist
    inverse = 1.0 / dist
    return jnp.cos(turn) * inverse, jnp.sin(turn) * inverse


def put_complex(ref, re, im):
    half = re.shape[0]
    ref[:half, :half] = re
    ref[:half, half:] = im
    ref[half:, :half] = -im
    ref[half:, half:] = re


def kernel(
    inc, leaf, con, skel, rank_in, core, out,
    x, a, idx, rank, cont, cq, et, es0, es1, g0h, g0l, g1h, g1l, cc,
    ws, wr, cs, cr, ss, sr, v, held,
    lsem, xsend, xrecv, csend, crecv, wsend, wrecv, ksend, krecv, ssend, srecv,
):
    fields, leafs = inc.shape[1], inc.shape[2]
    kmax = skel.shape[2]
    rows = leaf.shape[2]
    box = lax.axis_index("box")
    me = lax.axis_index("field")
    right, left, across = (me + 1) % 4, (me + 3) % 4, (me + 2) % 4
    box1 = box + 1 - 2 * (box % 2)
    box2 = box + 2 - 4 * ((box // 2) % 2)
    box3 = box2 + 1 - 2 * (box % 2)
    quad = box % 4

    def local(src, dst, at):
        copy = pltpu.make_async_copy(src, dst, lsem.at[at])
        copy.start()
        return copy

    load_idx = [
        local(skel.at[who], idx.at[at], at) for at, who in enumerate((box, box1, box2))
    ]
    load_rank = local(rank_in, rank, 3)
    load_con = local(con, cont, 4)
    load_x = local(inc, x, 5)
    load_a = local(leaf.at[0], a.at[me], 6)
    load_c = local(core, cq.at[quad], 7)

    barrier = pltpu.get_barrier_semaphore()
    for peer in ((box, right), (box, left), (box1, me), (box2, me), (box3, me)):
        pl.semaphore_signal(barrier, inc=1, device_id=peer, device_id_type=MESH)
    pl.semaphore_wait(barrier, 5)

    def remote(src, dst, send, recv, peer):
        copy = pltpu.make_async_remote_copy(
            src_ref=src, dst_ref=dst, send_sem=send, recv_sem=recv,
            device_id=peer, device_id_type=MESH,
        )
        copy.start()
        return copy

    def ring(src, owner, part, at, to):
        return remote(src, a.at[owner, part], xsend.at[at], xrecv.at[at], (box, to))

    from_left_re = ring(leaf.at[0, 0], me, 0, 0, right)
    from_right_im = ring(leaf.at[0, 1], me, 1, 3, left)
    from_left_im = ring(leaf.at[0, 1], me, 1, 1, right)
    from_right_re = ring(leaf.at[0, 0], me, 0, 4, left)
    cores = [
        remote(core, cq.at[quad], csend.at[at], crecv.at[at], (who, me))
        for at, who in enumerate((box1, box2, box3))
    ]

    for copy in load_idx:
        copy.wait()
    load_rank.wait()
    load_con.wait()
    own = idx[0]
    own0, own1 = own[0:1], own[1:2]
    far0, far1 = idx[1][0:1], idx[2][1:2]
    at_box = lax.broadcasted_iota(jnp.int32, rank.shape, 1) == box
    ranks = jnp.sum(jnp.where(at_box, rank[...].astype(F32), 0.0), axis=1, keepdims=True)
    at_k = lax.broadcasted_iota(jnp.int32, (1, kmax), 1)
    in0 = at_k.astype(F32) < ranks[0:1]
    in1 = at_k.astype(F32) < ranks[1:2]
    pick0 = jnp.where(in0, own0, -1)
    pick1 = jnp.where(in1, own1, -1)
    pick1_too = jnp.where(in1, own1, -2)
    table = jnp.concatenate([pick0, pick1, far0, far1, own0, own0, own0, own0], axis=0)
    columns = jnp.transpose(table.astype(F32)).astype(jnp.int32)

    both = jnp.concatenate([pick0, pick1], axis=1)
    at_n = lax.broadcasted_iota(jnp.int32, (rows, 2 * kmax), 0)
    contrast = cont[...]
    c_high = contrast.astype(BF16).astype(F32)
    c_mid = (contrast - c_high).astype(BF16).astype(F32)
    c_low = contrast - c_high - c_mid
    zero = jnp.zeros((5, leafs), F32)
    c_rows = jnp.concatenate([c_high, c_mid, c_low, zero], axis=0).astype(BF16)
    weight = jnp.zeros((8, 2 * kmax), F32)
    for block in range(leafs // rows):
        hit = jnp.where(at_n + block * rows == both, 1.0, 0.0).astype(BF16)
        et[block, :rows] = hit
        et[block, rows:] = hit
        weight = weight + dot_nn(c_rows[:, block * rows : (block + 1) * rows], hit)
    weight = jnp.sum(weight, axis=0, keepdims=True)
    q0, q1 = weight[:, :kmax], weight[:, kmax:]

    def block_of(owner, start, size, first):
        matrix = a[owner].reshape(2 * rows, leafs)
        at_f = pl.ds(start, size)
        by_re = dot_nt(x[0, at_f, :], matrix)
        by_im = dot_nt(x[1, at_f, :], matrix)
        y_re = by_re[:, :rows] - by_im[:, rows:]
        y_im = by_re[:, rows:] + by_im[:, :rows]
        at_cols = pl.ds(pl.multiple_of(owner * rows, rows), rows)
        out[0, at_f, at_cols] = y_re
        out[1, at_f, at_cols] = y_im
        high, low = halves(jnp.concatenate([y_re, y_im], axis=0))
        picked = dot_nn(jnp.concatenate([high, low], axis=1), et[owner])
        if not first:
            picked = picked + jnp.concatenate([v[0, at_f, :], v[1, at_f, :]], axis=0)
        v[0, at_f, :] = picked[:size]
        v[1, at_f, :] = picked[size:]

    def whole_block(owner, first):
        for start in range(0, fields, 2 * CHUNK):
            block_of(owner, start, 2 * CHUNK, first)

    load_x.wait()
    load_a.wait()
    whole_block(me, True)

    g_re, g_im = green(columns[:, 2:3], own0, 8 * (box1 - box))
    re_h, re_l = halves(g_re)
    im_h, im_l = halves(g_im)
    put_complex(g0h, re_h, im_h)
    put_complex(g0l, re_l, im_l)

    from_left_re.wait_recv()
    on_right = ring(a.at[left, 0], left, 0, 2, right)
    from_right_im.wait_recv()
    on_left = ring(a.at[right, 1], right, 1, 5, left)

    at_l = lax.broadcasted_iota(jnp.int32, (1, leafs), 1)
    lanes = jnp.concatenate([at_l, pick1_too], axis=1)
    es0[...] = jnp.where(columns[:, 0:1] == lanes, 1.0, 0.0).astype(BF16)
    es1[...] = jnp.where(columns[:, 1:2] == lanes, 1.0, 0.0).astype(BF16)

    from_left_im.wait_recv()
    whole_block(left, False)
    from_right_re.wait_recv()
    whole_block(right, False)

    g_re, g_im = green(columns[:, 3:4], own1, 8 * (box2 - box))
    re_h, re_l = halves(g_re)
    im_h, im_l = halves(g_im)
    put_complex(g1h, re_h, im_h)
    put_complex(g1l, re_l, im_l)

    load_c.wait()
    for copy in cores:
        copy.wait_recv()
    c_re = jnp.concatenate([cq[at, 0] for at in range(4)], axis=0)
    c_im = jnp.concatenate([cq[at, 1] for at in range(4)], axis=0)
    put_complex(cc, c_re, c_im)

    def first_stage(c):
        start = c * CHUNK
        at_f = pl.ds(start, CHUNK)
        block_of(across, start, CHUNK, False)
        value = jnp.concatenate([v[0, at_f, :kmax] * q0, v[1, at_f, :kmax] * q0], axis=1)
        ws[c, 0], ws[c, 1] = halves(value)
        return remote(ws.at[c], wr.at[c], wsend.at[c], wrecv.at[c], (box1, me))

    def coupled(high, low, ref_h, ref_l):
        main = dot_nn(jnp.concatenate([high, low], axis=0), ref_h[...])
        return main[:CHUNK] + main[CHUNK:] + dot_nn(high, ref_l[...])

    def spread(value, ref):
        high, low = halves(jnp.concatenate([value[:, :kmax], value[:, kmax:]], axis=0))
        both_parts = dot_nn(jnp.concatenate([high, low], axis=0), ref)
        return both_parts[: 2 * CHUNK] + both_parts[2 * CHUNK :]

    def second_stage(c, arriving):
        at_f = pl.ds(c * CHUNK, CHUNK)
        arriving.wait_recv()
        pushed = coupled(wr[c, 0], wr[c, 1], g0h, g0l)
        moved = spread(pushed, es0[...])
        v_re = v[0, at_f, kmax:] - moved[:CHUNK, leafs:]
        v_im = v[1, at_f, kmax:] - moved[CHUNK:, leafs:]
        v[0, at_f, kmax:] = v_re
        v[1, at_f, kmax:] = v_im
        most = jnp.max(jnp.maximum(jnp.abs(v_re), jnp.abs(v_im)), axis=0, keepdims=True)
        scale = TOP / jnp.maximum(most, 1e-30)
        code_re = jnp.round(v_re * scale).astype(jnp.int32).astype(jnp.int16)
        code_im = jnp.round(v_im * scale).astype(jnp.int32).astype(jnp.int16)
        cs[c, :, :kmax] = code_re
        cs[c, :, kmax:] = code_im
        step = jnp.maximum(most, 1e-30) * (1.0 / TOP) * q1
        ss[c] = jnp.broadcast_to(step, (8, kmax))
        codes = remote(cs.at[c], cr.at[c], ksend.at[c], krecv.at[c], (box2, me))
        steps = remote(ss.at[c], sr.at[c], ssend.at[c], srecv.at[c], (box2, me))
        out[0, at_f, :] = out[0, at_f, :] - moved[:CHUNK, :leafs]
        out[1, at_f, :] = out[1, at_f, :] - moved[CHUNK:, :leafs]
        return codes, steps

    def third_stage(c, codes, steps):
        at_f = pl.ds(c * CHUNK, CHUNK)
        codes.wait_recv()
        steps.wait_recv()
        step = sr[c][0:1]
        step = jnp.concatenate([step, step], axis=1)
        high, low = halves(cr[c].astype(jnp.int32).astype(F32) * step)
        pushed = coupled(high, low, g1h, g1l)
        held[...] = pushed
        again = spread(pushed, es1[:, leafs:])
        coarse = jnp.concatenate(
            [v[0, at_f, kmax:] - again[:CHUNK], v[1, at_f, kmax:] - again[CHUNK:]], axis=1
        )
        high, low = halves(coarse)
        main = dot_nn(jnp.concatenate([high, low], axis=0), cc[...])
        total = held[...] + (main[:CHUNK] + main[CHUNK:])
        moved = spread(total, es1[:, :leafs])
        out[0, at_f, :] = out[0, at_f, :] - moved[:CHUNK]
        out[1, at_f, :] = out[1, at_f, :] - moved[CHUNK:]

    on_right.wait_recv()
    on_left.wait_recv()
    chunks = fields // CHUNK
    sent = []
    codes = []
    for c in range(chunks + 1):
        if c < chunks:
            sent.append(first_stage(c))
        if c > 0:
            codes.append(second_stage(c - 1, sent[c - 1]))
    for c in range(chunks):
        third_stage(c, *codes[c])

    for copy in (from_left_re, from_left_im, from_right_im, from_right_re, on_right, on_left):
        copy.wait_send()
    for copy in cores + sent:
        copy.wait_send()
    for pair in codes:
        for copy in pair:
            copy.wait_send()


def body(incident, leaf_inverse, contrast, skel_index, ranks, top_core):
    _, fields, leafs = incident.shape
    rows = leaf_inverse.shape[2]
    kmax = skel_index.shape[2]
    boxes, kq = ranks.shape[0], top_core.shape[2]
    chunks = fields // CHUNK
    wide = 2 * kmax
    dma = pltpu.SemaphoreType.DMA
    return pl.pallas_call(
        kernel,
        out_shape=jax.ShapeDtypeStruct(incident.shape, F32),
        in_specs=[pl.BlockSpec(memory_space=pltpu.HBM)] * 6,
        out_specs=pl.BlockSpec(memory_space=pltpu.VMEM),
        scratch_shapes=[
            pltpu.VMEM((2, fields, leafs), BF16),
            pltpu.VMEM((4, 2, rows, leafs), BF16),
            pltpu.VMEM((3, 2, kmax), jnp.int32),
            pltpu.VMEM((2, boxes), jnp.int32),
            pltpu.VMEM((1, leafs), F32),
            pltpu.VMEM((4, 2, kq, kmax), BF16),
            pltpu.VMEM((4, 2 * rows, wide), BF16),
            pltpu.VMEM((kmax, leafs + kmax), BF16),
            pltpu.VMEM((kmax, leafs + kmax), BF16),
            pltpu.VMEM((wide, wide), BF16),
            pltpu.VMEM((wide, wide), BF16),
            pltpu.VMEM((wide, wide), BF16),
            pltpu.VMEM((wide, wide), BF16),
            pltpu.VMEM((wide, wide), BF16),
            pltpu.VMEM((chunks, 2, CHUNK, wide), BF16),
            pltpu.VMEM((chunks, 2, CHUNK, wide), BF16),
            pltpu.VMEM((chunks, CHUNK, wide), jnp.int16),
            pltpu.VMEM((chunks, CHUNK, wide), jnp.int16),
            pltpu.VMEM((chunks, 8, kmax), F32),
            pltpu.VMEM((chunks, 8, kmax), F32),
            pltpu.VMEM((2, fields, wide), F32),
            pltpu.VMEM((CHUNK, wide), F32),
            dma((8,)), dma((6,)), dma((6,)), dma((3,)), dma((3,)),
            dma((chunks,)), dma((chunks,)), dma((chunks,)), dma((chunks,)),
            dma((chunks,)), dma((chunks,)),
        ],
        compiler_params=pltpu.CompilerParams(
            collective_id=0, has_side_effects=True, vmem_limit_bytes=48 << 20
        ),
        name="solve",
    )(
        *(
            pltpu.with_memory_space_constraint(value, pltpu.HBM)
            for value in (
                incident,
                leaf_inverse,
                contrast.reshape(1, leafs),
                skel_index,
                ranks.T,
                jnp.swapaxes(top_core, 1, 2),
            )
        )
    )


def solution(mesh):
    return jax.shard_map(
        body,
        mesh=mesh,
        in_specs=(
            P(None, "field", "box"),
            P("box", None, "field", None),
            P("box"),
            P(),
            P(),
            P(None, None, "box"),
        ),
        out_specs=P(None, "field", "box"),
        check_vma=False,
    )
```

```python
import functools

import jax
import jax.numpy as jnp
from jax import lax
from jax.experimental import pallas as pl
from jax.experimental.pallas import tpu as pltpu
from jax.sharding import PartitionSpec as P

MESH = pl.DeviceIdType.MESH
WAVENUM = 0.7
F32 = jnp.float32
BF16 = jnp.bfloat16
CHUNKS = (64, 128, 128, 128, 64)
TOP = 32767.0


def dot_nn(lhs, rhs):
    return lax.dot_general(lhs, rhs, (((1,), (0,)), ((), ())), preferred_element_type=F32)


def dot_nt(lhs, rhs):
    return lax.dot_general(lhs, rhs, (((1,), (1,)), ((), ())), preferred_element_type=F32)


def halves(value):
    high = value.astype(BF16)
    low = (value - high.astype(F32)).astype(BF16)
    return high, low


def grid_of(index):
    return index & 7, (index >> 3) & 7, index >> 6


def green(far_col, own_row, apart):
    fx, fy, fz = grid_of(far_col)
    ox, oy, oz = grid_of(own_row)
    dx = (fx - ox + apart).astype(F32)
    dy = (fy - oy).astype(F32)
    dz = (fz - oz).astype(F32)
    dist = jnp.sqrt(dx * dx + dy * dy + dz * dz)
    turn = WAVENUM * dist
    inverse = 1.0 / dist
    return jnp.cos(turn) * inverse, jnp.sin(turn) * inverse


def put_complex(ref, re, im):
    half = re.shape[0]
    ref[:half, :half] = re
    ref[:half, half:] = im
    ref[half:, :half] = -im
    ref[half:, half:] = re


def remote(src, dst, send, recv, peer):
    copy = pltpu.make_async_remote_copy(
        src_ref=src, dst_ref=dst, send_sem=send, recv_sem=recv,
        device_id=peer, device_id_type=MESH,
    )
    copy.start()
    return copy


def meet(peers):
    barrier = pltpu.get_barrier_semaphore()
    for peer in peers:
        pl.semaphore_signal(barrier, inc=1, device_id=peer, device_id_type=MESH)
    return barrier


def places():
    box = lax.axis_index("box")
    me = lax.axis_index("field")
    return box, me, box + 1 - 2 * (box % 2), box + 2 - 4 * ((box // 2) % 2)


def leaf_part(x, matrix, picks, at_f):
    rows = matrix.shape[0] // 2
    by_re = dot_nt(x[0, at_f, :], matrix)
    by_im = dot_nt(x[1, at_f, :], matrix)
    y_re = by_re[:, :rows] - by_im[:, rows:]
    y_im = by_re[:, rows:] + by_im[:, :rows]
    high, low = halves(jnp.concatenate([y_re, y_im], axis=0))
    return y_re, y_im, dot_nn(jnp.concatenate([high, low], axis=1), picks)


def gather_kernel(
    inc, leaf, con, skel, rank_in,
    y, v, x, a, et, es0, es1, g0h, g0l, g1h, g1l, weights,
    idx, rank, cont, lsem, xsend, xrecv,
):
    fields, leafs = inc.shape[1], inc.shape[2]
    kmax = skel.shape[2]
    rows = leaf.shape[2]
    box, me, box1, box2 = places()
    right, left = (me + 1) % 4, (me + 3) % 4

    def local(src, dst, at):
        copy = pltpu.make_async_copy(src, dst, lsem.at[at])
        copy.start()
        return copy

    barrier = meet(((box, right), (box, left)))
    load_idx = [
        local(skel.at[who], idx.at[at], at) for at, who in enumerate((box, box1, box2))
    ]
    load_rank = local(rank_in, rank, 3)
    load_con = local(con, cont, 4)
    load_x = local(inc, x, 5)
    load_a = local(leaf.at[0], a.at[me], 6)
    pl.semaphore_wait(barrier, 2)

    def ring(src, owner, part, at, to):
        return remote(src, a.at[owner, part], xsend.at[at], xrecv.at[at], (box, to))

    from_left_re = ring(leaf.at[0, 0], me, 0, 0, right)
    from_right_im = ring(leaf.at[0, 1], me, 1, 3, left)
    from_left_im = ring(leaf.at[0, 1], me, 1, 1, right)
    from_right_re = ring(leaf.at[0, 0], me, 0, 4, left)

    for copy in load_idx:
        copy.wait()
    load_rank.wait()
    load_con.wait()
    own = idx[0]
    own0, own1 = own[0:1], own[1:2]
    far0, far1 = idx[1][0:1], idx[2][1:2]
    at_box = lax.broadcasted_iota(jnp.int32, rank.shape, 1) == box
    ranks = jnp.sum(jnp.where(at_box, rank[...].astype(F32), 0.0), axis=1, keepdims=True)
    at_k = lax.broadcasted_iota(jnp.int32, (1, kmax), 1)
    in0 = at_k.astype(F32) < ranks[0:1]
    in1 = at_k.astype(F32) < ranks[1:2]
    pick0 = jnp.where(in0, own0, -1)
    pick1 = jnp.where(in1, own1, -1)
    pick1_too = jnp.where(in1, own1, -2)
    table = jnp.concatenate([pick0, pick1, far0, far1, own0, own0, own0, own0], axis=0)
    columns = jnp.transpose(table.astype(F32)).astype(jnp.int32)

    both = jnp.concatenate([pick0, pick1], axis=1)
    at_n = lax.broadcasted_iota(jnp.int32, (rows, 2 * kmax), 0)
    contrast = cont[...]
    c_high = contrast.astype(BF16).astype(F32)
    c_mid = (contrast - c_high).astype(BF16).astype(F32)
    c_low = contrast - c_high - c_mid
    zero = jnp.zeros((5, leafs), F32)
    c_rows = jnp.concatenate([c_high, c_mid, c_low, zero], axis=0).astype(BF16)
    weight = jnp.zeros((8, 2 * kmax), F32)
    for block in range(leafs // rows):
        hit = jnp.where(at_n + block * rows == both, 1.0, 0.0).astype(BF16)
        et[block, :rows] = hit
        et[block, rows:] = hit
        weight = weight + dot_nn(c_rows[:, block * rows : (block + 1) * rows], hit)
    weight = jnp.sum(weight, axis=0, keepdims=True)
    weights[...] = jnp.broadcast_to(weight, weights.shape)

    def whole_block(owner, first):
        matrix = a[owner].reshape(2 * rows, leafs)
        size = min(256, fields)
        for start in range(0, fields, size):
            at_f = pl.ds(start, size)
            y_re, y_im, picked = leaf_part(x, matrix, et[owner], at_f)
            at_cols = pl.ds(pl.multiple_of(owner * rows, rows), rows)
            y[0, at_f, at_cols] = y_re
            y[1, at_f, at_cols] = y_im
            if not first:
                picked = picked + jnp.concatenate([v[0, at_f, :], v[1, at_f, :]], axis=0)
            v[0, at_f, :] = picked[:size]
            v[1, at_f, :] = picked[size:]

    load_x.wait()
    load_a.wait()
    whole_block(me, True)

    g_re, g_im = green(columns[:, 2:3], own0, 8 * (box1 - box))
    re_h, re_l = halves(g_re)
    im_h, im_l = halves(g_im)
    put_complex(g0h, re_h, im_h)
    put_complex(g0l, re_l, im_l)

    from_left_re.wait_recv()
    on_right = ring(a.at[left, 0], left, 0, 2, right)
    from_right_im.wait_recv()
    on_left = ring(a.at[right, 1], right, 1, 5, left)

    at_l = lax.broadcasted_iota(jnp.int32, (1, leafs), 1)
    lanes = jnp.concatenate([at_l, pick1_too], axis=1)
    es0[...] = jnp.where(columns[:, 0:1] == lanes, 1.0, 0.0).astype(BF16)
    es1[...] = jnp.where(columns[:, 1:2] == lanes, 1.0, 0.0).astype(BF16)

    from_left_im.wait_recv()
    whole_block(left, False)
    from_right_re.wait_recv()
    whole_block(right, False)

    g_re, g_im = green(columns[:, 3:4], own1, 8 * (box2 - box))
    re_h, re_l = halves(g_re)
    im_h, im_l = halves(g_im)
    put_complex(g1h, re_h, im_h)
    put_complex(g1l, re_l, im_l)

    on_right.wait_recv()
    on_left.wait_recv()
    for copy in (from_left_re, from_left_im, from_right_im, from_right_re, on_right, on_left):
        copy.wait_send()


def merge_kernel(
    y, v_in, x, a, et, es0, es1, g0h, g0l, g1h, g1l, weights, core, out,
    cq, cc, ws, wr, cs, cr, ss, sr, v, held,
    lsem, csend, crecv, wsend, wrecv, ksend, krecv, ssend, srecv,
):
    leafs = y.shape[2]
    kmax = cc.shape[0] // 2
    rows = a.shape[2]
    box, me, box1, box2 = places()
    across = (me + 2) % 4
    quad, quad2 = box % 4, box2 % 4
    barrier = meet(((box1, me), (box2, me)))
    load_c = pltpu.make_async_copy(core, cq.at[quad], lsem)
    load_c.start()
    q0, q1 = weights[0:1, :kmax], weights[0:1, kmax:]
    starts = [sum(CHUNKS[:c]) for c in range(len(CHUNKS))]

    def first_compute(c):
        size = CHUNKS[c]
        at_f = pl.ds(starts[c], size)
        matrix = a[across].reshape(2 * rows, leafs)
        y_re, y_im, picked = leaf_part(x, matrix, et[across], at_f)
        at_cols = pl.ds(pl.multiple_of(across * rows, rows), rows)
        v_re = v_in[0, at_f, :] + picked[:size]
        v_im = v_in[1, at_f, :] + picked[size:]
        v[0, at_f, :] = v_re[:, kmax:]
        v[1, at_f, :] = v_im[:, kmax:]
        value = jnp.concatenate([v_re[:, :kmax] * q0, v_im[:, :kmax] * q0], axis=1)
        ws[0, at_f, :], ws[1, at_f, :] = halves(value)
        out[0, at_f, :] = y[0, at_f, :]
        out[1, at_f, :] = y[1, at_f, :]
        out[0, at_f, at_cols] = y_re
        out[1, at_f, at_cols] = y_im

    def first_send(c):
        at_f = pl.ds(starts[c], CHUNKS[c])
        return remote(ws.at[:, at_f], wr.at[:, at_f], wsend.at[c], wrecv.at[c], (box1, me))

    def coupled(high, low, ref_h, ref_l):
        size = high.shape[0]
        main = dot_nn(jnp.concatenate([high, low], axis=0), ref_h[...])
        return main[:size] + main[size:] + dot_nn(high, ref_l[...])

    def spread(value, matrix):
        size = 2 * value.shape[0]
        high, low = halves(jnp.concatenate([value[:, :kmax], value[:, kmax:]], axis=0))
        parts = dot_nn(jnp.concatenate([high, low], axis=0), matrix)
        return parts[:size] + parts[size:]

    def second_stage(c, arriving):
        size = CHUNKS[c]
        at_f = pl.ds(starts[c], size)
        arriving.wait_recv()
        pushed = coupled(wr[0, at_f, :], wr[1, at_f, :], g0h, g0l)
        moved = spread(pushed, es0[...])
        v_re = v[0, at_f, :] - moved[:size, leafs:]
        v_im = v[1, at_f, :] - moved[size:, leafs:]
        v[0, at_f, :] = v_re
        v[1, at_f, :] = v_im
        most = jnp.max(jnp.maximum(jnp.abs(v_re), jnp.abs(v_im)), axis=0, keepdims=True)
        most = jnp.maximum(most, 1e-30)
        scale = TOP / most
        cs[at_f, :kmax] = jnp.round(v_re * scale).astype(jnp.int32).astype(jnp.int16)
        cs[at_f, kmax:] = jnp.round(v_im * scale).astype(jnp.int32).astype(jnp.int16)
        ss[c] = jnp.broadcast_to(most * (1.0 / TOP) * q1, (8, kmax))
        codes = remote(cs.at[at_f], cr.at[at_f], ksend.at[c], krecv.at[c], (box2, me))
        steps = remote(ss.at[c], sr.at[c], ssend.at[c], srecv.at[c], (box2, me))
        out[0, at_f, :] = out[0, at_f, :] - moved[:size, :leafs]
        out[1, at_f, :] = out[1, at_f, :] - moved[size:, :leafs]
        return codes, steps

    def third_stage(c, codes, steps):
        size = CHUNKS[c]
        at_f = pl.ds(starts[c], size)
        codes.wait_recv()
        steps.wait_recv()
        step = sr[c][0:1]
        step = jnp.concatenate([step, step], axis=1)
        high, low = halves(cr[at_f, :].astype(jnp.int32).astype(F32) * step)
        pushed = coupled(high, low, g1h, g1l)
        held[:size] = pushed
        again = spread(pushed, es1[:, leafs:])
        coarse = jnp.concatenate(
            [v[0, at_f, :] - again[:size], v[1, at_f, :] - again[size:]], axis=1
        )
        high, low = halves(coarse)
        main = dot_nn(jnp.concatenate([high, low], axis=0), cc[...])
        total = held[:size] + (main[:size] + main[size:])
        moved = spread(total, es1[:, :leafs])
        out[0, at_f, :] = out[0, at_f, :] - moved[:size]
        out[1, at_f, :] = out[1, at_f, :] - moved[size:]

    chunks = len(CHUNKS)
    first_compute(0)
    pl.semaphore_wait(barrier, 2)
    sent = [first_send(0)]
    core2 = remote(core, cq.at[quad], csend.at[0], crecv.at[0], (box2, me))
    core1 = remote(core, cq.at[quad], csend.at[1], crecv.at[1], (box1, me))
    codes = []
    for c in range(1, chunks + 1):
        if c < chunks:
            first_compute(c)
            sent.append(first_send(c))
        codes.append(second_stage(c - 1, sent[c - 1]))
        if c == 2:
            core2.wait_recv()
            core3 = remote(cq.at[quad2], cq.at[quad2], csend.at[2], crecv.at[2], (box1, me))

    load_c.wait()
    core1.wait_recv()
    core3.wait_recv()
    c_re = jnp.concatenate([cq[at, 0] for at in range(4)], axis=0)
    c_im = jnp.concatenate([cq[at, 1] for at in range(4)], axis=0)
    put_complex(cc, c_re, c_im)
    for c in range(chunks):
        third_stage(c, *codes[c])

    for copy in [core1, core2, core3] + sent:
        copy.wait_send()
    for pair in codes:
        for copy in pair:
            copy.wait_send()


def body(incident, leaf_inverse, contrast, skel_index, ranks, top_core):
    _, fields, leafs = incident.shape
    rows = leaf_inverse.shape[2]
    kmax = skel_index.shape[2]
    boxes, kq = ranks.shape[0], top_core.shape[2]
    chunks = len(CHUNKS)
    wide = 2 * kmax
    dma = pltpu.SemaphoreType.DMA
    vmem = pl.BlockSpec(memory_space=pltpu.VMEM)
    hbm = pl.BlockSpec(memory_space=pltpu.HBM)
    made = [
        ((2, fields, leafs), F32),
        ((2, fields, wide), F32),
        ((2, fields, leafs), BF16),
        ((4, 2, rows, leafs), BF16),
        ((4, 2 * rows, wide), BF16),
        ((kmax, leafs + kmax), BF16),
        ((kmax, leafs + kmax), BF16),
        ((wide, wide), BF16),
        ((wide, wide), BF16),
        ((wide, wide), BF16),
        ((wide, wide), BF16),
        ((8, wide), F32),
    ]

    def in_hbm(value):
        return pltpu.with_memory_space_constraint(value, pltpu.HBM)

    state = pl.pallas_call(
        gather_kernel,
        out_shape=[jax.ShapeDtypeStruct(*each) for each in made],
        in_specs=[hbm] * 5,
        out_specs=[vmem] * len(made),
        scratch_shapes=[
            pltpu.VMEM((3, 2, kmax), jnp.int32),
            pltpu.VMEM((2, boxes), jnp.int32),
            pltpu.VMEM((1, leafs), F32),
            dma((7,)), dma((6,)), dma((6,)),
        ],
        compiler_params=pltpu.CompilerParams(
            collective_id=0, has_side_effects=True, vmem_limit_bytes=24 << 20
        ),
        name="gather",
    )(*map(in_hbm, (incident, leaf_inverse, contrast.reshape(1, leafs), skel_index, ranks.T)))
    return pl.pallas_call(
        merge_kernel,
        out_shape=jax.ShapeDtypeStruct(incident.shape, F32),
        in_specs=[vmem] * len(made) + [hbm],
        out_specs=vmem,
        scratch_shapes=[
            pltpu.VMEM((4, 2, kq, kmax), BF16),
            pltpu.VMEM((wide, wide), BF16),
            pltpu.VMEM((2, fields, wide), BF16),
            pltpu.VMEM((2, fields, wide), BF16),
            pltpu.VMEM((fields, wide), jnp.int16),
            pltpu.VMEM((fields, wide), jnp.int16),
            pltpu.VMEM((chunks, 8, kmax), F32),
            pltpu.VMEM((chunks, 8, kmax), F32),
            pltpu.VMEM((2, fields, kmax), F32),
            pltpu.VMEM((max(CHUNKS), wide), F32),
            dma, dma((3,)), dma((3,)),
            dma((chunks,)), dma((chunks,)), dma((chunks,)), dma((chunks,)),
            dma((chunks,)), dma((chunks,)),
        ],
        compiler_params=pltpu.CompilerParams(
            collective_id=1, has_side_effects=True, vmem_limit_bytes=28 << 20
        ),
        name="merge",
    )(*state, in_hbm(jnp.swapaxes(top_core, 1, 2)))


def solution(mesh):
    return jax.shard_map(
        body,
        mesh=mesh,
        in_specs=(
            P(None, "field", "box"),
            P("box", None, "field", None),
            P("box"),
            P(),
            P(),
            P(None, None, "box"),
        ),
        out_specs=P(None, "field", "box"),
        check_vma=False,
    )
```

```python
import functools

import jax
import jax.numpy as jnp
from jax import lax
from jax.experimental import pallas as pl
from jax.experimental.pallas import tpu as pltpu
from jax.sharding import PartitionSpec as P

MESH = pl.DeviceIdType.MESH
WAVENUM = 0.7
F32 = jnp.float32
BF16 = jnp.bfloat16
CHUNKS = (64, 128, 128, 128, 64)
TOP = 32767.0


def dot_nn(lhs, rhs):
    return lax.dot_general(lhs, rhs, (((1,), (0,)), ((), ())), preferred_element_type=F32)


def dot_nt(lhs, rhs):
    return lax.dot_general(lhs, rhs, (((1,), (1,)), ((), ())), preferred_element_type=F32)


def halves(value):
    high = value.astype(BF16)
    low = (value - high.astype(F32)).astype(BF16)
    return high, low


def grid_of(index):
    return tuple(part.astype(F32) for part in (index & 7, (index >> 3) & 7, index >> 6))


def green(far_col, own_row, apart):
    fx, fy, fz = grid_of(far_col)
    ox, oy, oz = grid_of(own_row)
    dx = fx - (ox - apart)
    dy = fy - oy
    dz = fz - oz
    square = dx * dx + dy * dy + dz * dz
    inverse = lax.rsqrt(square)
    inverse = inverse * (1.5 - 0.5 * square * inverse * inverse)
    turn = WAVENUM * (square * inverse)
    quarter = jnp.floor(turn * 0.6366197723675814 + 0.5)
    rest = (turn - quarter * 1.5703125) - quarter * 4.838267948966e-4
    sq = rest * rest
    sine = rest + rest * sq * (
        -1.6666654611e-1 + sq * (8.3321608736e-3 - sq * 1.9515295891e-4)
    )
    cosine = 1.0 + sq * (
        -0.5 + sq * (4.166664568298827e-2 + sq * (-1.388731625493765e-3 + sq * 2.443315711809948e-5))
    )
    turns = quarter.astype(jnp.int32)
    odd = (turns & 1) == 1
    minus = -inverse
    re = jnp.where(odd, sine, cosine) * jnp.where(((turns + 1) & 2) == 0, inverse, minus)
    im = jnp.where(odd, cosine, sine) * jnp.where((turns & 2) == 0, inverse, minus)
    return re, im


def put_complex(ref, re, im):
    half = re.shape[0]
    ref[:half, :half] = re
    ref[:half, half:] = im
    ref[half:, :half] = -im
    ref[half:, half:] = re


def remote(src, dst, send, recv, peer):
    copy = pltpu.make_async_remote_copy(
        src_ref=src, dst_ref=dst, send_sem=send, recv_sem=recv,
        device_id=peer, device_id_type=MESH,
    )
    copy.start()
    return copy


def meet(peers):
    barrier = pltpu.get_barrier_semaphore()
    for peer in peers:
        pl.semaphore_signal(barrier, inc=1, device_id=peer, device_id_type=MESH)
    return barrier


def places():
    box = lax.axis_index("box")
    me = lax.axis_index("field")
    return box, me, box + 1 - 2 * (box % 2), box + 2 - 4 * ((box // 2) % 2)


def leaf_part(x, matrix, picks, at_f):
    rows = matrix.shape[0] // 2
    by_re = dot_nt(x[0, at_f, :], matrix)
    by_im = dot_nt(x[1, at_f, :], matrix)
    y_re = by_re[:, :rows] - by_im[:, rows:]
    y_im = by_re[:, rows:] + by_im[:, :rows]
    high, low = halves(jnp.concatenate([y_re, y_im], axis=0))
    return y_re, y_im, dot_nn(jnp.concatenate([high, low], axis=1), picks)


def gather_kernel(
    inc, leaf, con, skel, rank_in,
    y, v, x, a, et, es0, es1, g0h, g0l, g1h, g1l, weights,
    idx, rank, cont, lsem, xsend, xrecv,
):
    fields, leafs = inc.shape[1], inc.shape[2]
    kmax = skel.shape[2]
    rows = leaf.shape[2]
    box, me, box1, box2 = places()
    right, left = (me + 1) % 4, (me + 3) % 4

    def local(src, dst, at):
        copy = pltpu.make_async_copy(src, dst, lsem.at[at])
        copy.start()
        return copy

    barrier = meet(((box, right), (box, left)))
    load_idx = [
        local(skel.at[who], idx.at[at], at) for at, who in enumerate((box, box1, box2))
    ]
    load_rank = local(rank_in, rank, 3)
    load_con = local(con, cont, 4)
    load_x = local(inc, x, 5)
    load_a = local(leaf.at[0], a.at[me], 6)
    pl.semaphore_wait(barrier, 2)

    def ring(src, owner, part, at, to):
        return remote(src, a.at[owner, part], xsend.at[at], xrecv.at[at], (box, to))

    from_left_re = ring(leaf.at[0, 0], me, 0, 0, right)
    from_right_im = ring(leaf.at[0, 1], me, 1, 3, left)
    from_left_im = ring(leaf.at[0, 1], me, 1, 1, right)
    from_right_re = ring(leaf.at[0, 0], me, 0, 4, left)

    for copy in load_idx:
        copy.wait()
    load_rank.wait()
    load_con.wait()
    own = idx[0]
    own0, own1 = own[0:1], own[1:2]
    far0, far1 = idx[1][0:1], idx[2][1:2]
    at_box = lax.broadcasted_iota(jnp.int32, rank.shape, 1) == box
    ranks = jnp.sum(jnp.where(at_box, rank[...].astype(F32), 0.0), axis=1, keepdims=True)
    at_k = lax.broadcasted_iota(jnp.int32, (1, kmax), 1)
    in0 = at_k.astype(F32) < ranks[0:1]
    in1 = at_k.astype(F32) < ranks[1:2]
    pick0 = jnp.where(in0, own0, -1)
    pick1 = jnp.where(in1, own1, -1)
    pick1_too = jnp.where(in1, own1, -2)
    table = jnp.concatenate([pick0, pick1, far0, far1, own0, own0, own0, own0], axis=0)
    columns = jnp.transpose(table.astype(F32)).astype(jnp.int32)

    both = jnp.concatenate([pick0, pick1], axis=1)
    at_n = lax.broadcasted_iota(jnp.int32, (rows, 2 * kmax), 0)
    contrast = cont[...]
    c_high = contrast.astype(BF16).astype(F32)
    c_mid = (contrast - c_high).astype(BF16).astype(F32)
    c_low = contrast - c_high - c_mid
    zero = jnp.zeros((5, leafs), F32)
    c_rows = jnp.concatenate([c_high, c_mid, c_low, zero], axis=0).astype(BF16)
    weight = jnp.zeros((8, 2 * kmax), F32)
    for block in range(leafs // rows):
        hit = jnp.where(at_n + block * rows == both, 1.0, 0.0).astype(BF16)
        et[block, :rows] = hit
        et[block, rows:] = hit
        weight = weight + dot_nn(c_rows[:, block * rows : (block + 1) * rows], hit)
    weight = jnp.sum(weight, axis=0, keepdims=True)
    weights[...] = jnp.broadcast_to(weight, weights.shape)

    def whole_block(owner, first):
        matrix = a[owner].reshape(2 * rows, leafs)
        size = min(256, fields)
        for start in range(0, fields, size):
            at_f = pl.ds(start, size)
            y_re, y_im, picked = leaf_part(x, matrix, et[owner], at_f)
            at_cols = pl.ds(pl.multiple_of(owner * rows, rows), rows)
            y[0, at_f, at_cols] = y_re
            y[1, at_f, at_cols] = y_im
            if not first:
                picked = picked + jnp.concatenate([v[0, at_f, :], v[1, at_f, :]], axis=0)
            v[0, at_f, :] = picked[:size]
            v[1, at_f, :] = picked[size:]

    load_x.wait()
    load_a.wait()
    whole_block(me, True)

    g_re, g_im = green(columns[:, 2:3], own0, (8 * (box1 - box)).astype(F32))
    re_h, re_l = halves(g_re)
    im_h, im_l = halves(g_im)
    put_complex(g0h, re_h, im_h)
    put_complex(g0l, re_l, im_l)

    from_left_re.wait_recv()
    on_right = ring(a.at[left, 0], left, 0, 2, right)
    from_right_im.wait_recv()
    on_left = ring(a.at[right, 1], right, 1, 5, left)

    at_l = lax.broadcasted_iota(jnp.int32, (1, leafs), 1)
    lanes = jnp.concatenate([at_l, pick1_too], axis=1)
    es0[...] = jnp.where(columns[:, 0:1] == lanes, 1.0, 0.0).astype(BF16)
    es1[...] = jnp.where(columns[:, 1:2] == lanes, 1.0, 0.0).astype(BF16)

    from_left_im.wait_recv()
    whole_block(left, False)
    from_right_re.wait_recv()
    whole_block(right, False)

    g_re, g_im = green(columns[:, 3:4], own1, (8 * (box2 - box)).astype(F32))
    re_h, re_l = halves(g_re)
    im_h, im_l = halves(g_im)
    put_complex(g1h, re_h, im_h)
    put_complex(g1l, re_l, im_l)

    on_right.wait_recv()
    on_left.wait_recv()
    for copy in (from_left_re, from_left_im, from_right_im, from_right_re, on_right, on_left):
        copy.wait_send()


def merge_kernel(
    y, v_in, x, a, et, es0, es1, g0h, g0l, g1h, g1l, weights, core, out,
    cq, cc, ws, wr, cs, cr, ss, sr, v, held,
    lsem, csend, crecv, wsend, wrecv, ksend, krecv, ssend, srecv,
):
    leafs = y.shape[2]
    kmax = cc.shape[0] // 2
    rows = a.shape[2]
    box, me, box1, box2 = places()
    across = (me + 2) % 4
    quad, quad2 = box % 4, box2 % 4
    barrier = meet(((box1, me), (box2, me)))
    load_c = pltpu.make_async_copy(core, cq.at[quad], lsem)
    load_c.start()
    q0, q1 = weights[0:1, :kmax], weights[0:1, kmax:]
    starts = [sum(CHUNKS[:c]) for c in range(len(CHUNKS))]

    def first_compute(c):
        size = CHUNKS[c]
        at_f = pl.ds(starts[c], size)
        matrix = a[across].reshape(2 * rows, leafs)
        y_re, y_im, picked = leaf_part(x, matrix, et[across], at_f)
        at_cols = pl.ds(pl.multiple_of(across * rows, rows), rows)
        v_re = v_in[0, at_f, :] + picked[:size]
        v_im = v_in[1, at_f, :] + picked[size:]
        v[0, at_f, :] = v_re[:, kmax:]
        v[1, at_f, :] = v_im[:, kmax:]
        value = jnp.concatenate([v_re[:, :kmax] * q0, v_im[:, :kmax] * q0], axis=1)
        ws[0, at_f, :], ws[1, at_f, :] = halves(value)
        out[0, at_f, :] = y[0, at_f, :]
        out[1, at_f, :] = y[1, at_f, :]
        out[0, at_f, at_cols] = y_re
        out[1, at_f, at_cols] = y_im

    def first_send(c):
        at_f = pl.ds(starts[c], CHUNKS[c])
        return remote(ws.at[:, at_f], wr.at[:, at_f], wsend.at[c], wrecv.at[c], (box1, me))

    def coupled(high, low, ref_h, ref_l):
        size = high.shape[0]
        main = dot_nn(jnp.concatenate([high, low], axis=0), ref_h[...])
        return main[:size] + main[size:] + dot_nn(high, ref_l[...])

    def spread(value, matrix):
        size = 2 * value.shape[0]
        high, low = halves(jnp.concatenate([value[:, :kmax], value[:, kmax:]], axis=0))
        parts = dot_nn(jnp.concatenate([high, low], axis=0), matrix)
        return parts[:size] + parts[size:]

    def second_stage(c, arriving):
        size = CHUNKS[c]
        at_f = pl.ds(starts[c], size)
        arriving.wait_recv()
        pushed = coupled(wr[0, at_f, :], wr[1, at_f, :], g0h, g0l)
        moved = spread(pushed, es0[...])
        v_re = v[0, at_f, :] - moved[:size, leafs:]
        v_im = v[1, at_f, :] - moved[size:, leafs:]
        v[0, at_f, :] = v_re
        v[1, at_f, :] = v_im
        most = jnp.max(jnp.maximum(jnp.abs(v_re), jnp.abs(v_im)), axis=0, keepdims=True)
        most = jnp.maximum(most, 1e-30)
        scale = TOP / most
        cs[at_f, :kmax] = jnp.round(v_re * scale).astype(jnp.int32).astype(jnp.int16)
        cs[at_f, kmax:] = jnp.round(v_im * scale).astype(jnp.int32).astype(jnp.int16)
        ss[c] = jnp.broadcast_to(most * (1.0 / TOP) * q1, (8, kmax))
        codes = remote(cs.at[at_f], cr.at[at_f], ksend.at[c], krecv.at[c], (box2, me))
        steps = remote(ss.at[c], sr.at[c], ssend.at[c], srecv.at[c], (box2, me))
        out[0, at_f, :] = out[0, at_f, :] - moved[:size, :leafs]
        out[1, at_f, :] = out[1, at_f, :] - moved[size:, :leafs]
        return codes, steps

    def third_stage(c, codes, steps):
        size = CHUNKS[c]
        at_f = pl.ds(starts[c], size)
        codes.wait_recv()
        steps.wait_recv()
        step = sr[c][0:1]
        step = jnp.concatenate([step, step], axis=1)
        high, low = halves(cr[at_f, :].astype(jnp.int32).astype(F32) * step)
        pushed = coupled(high, low, g1h, g1l)
        held[:size] = pushed
        again = spread(pushed, es1[:, leafs:])
        coarse = jnp.concatenate(
            [v[0, at_f, :] - again[:size], v[1, at_f, :] - again[size:]], axis=1
        )
        high, low = halves(coarse)
        main = dot_nn(jnp.concatenate([high, low], axis=0), cc[...])
        total = held[:size] + (main[:size] + main[size:])
        moved = spread(total, es1[:, :leafs])
        out[0, at_f, :] = out[0, at_f, :] - moved[:size]
        out[1, at_f, :] = out[1, at_f, :] - moved[size:]

    chunks = len(CHUNKS)
    first_compute(0)
    pl.semaphore_wait(barrier, 2)
    sent = [first_send(0)]
    core2 = remote(core, cq.at[quad], csend.at[0], crecv.at[0], (box2, me))
    core1 = remote(core, cq.at[quad], csend.at[1], crecv.at[1], (box1, me))
    codes = []
    for c in range(1, chunks + 1):
        if c < chunks:
            first_compute(c)
            sent.append(first_send(c))
        codes.append(second_stage(c - 1, sent[c - 1]))
        if c == 2:
            core2.wait_recv()
            core3 = remote(cq.at[quad2], cq.at[quad2], csend.at[2], crecv.at[2], (box1, me))

    load_c.wait()
    core1.wait_recv()
    core3.wait_recv()
    c_re = jnp.concatenate([cq[at, 0] for at in range(4)], axis=0)
    c_im = jnp.concatenate([cq[at, 1] for at in range(4)], axis=0)
    put_complex(cc, c_re, c_im)
    for c in range(chunks):
        third_stage(c, *codes[c])

    for copy in [core1, core2, core3] + sent:
        copy.wait_send()
    for pair in codes:
        for copy in pair:
            copy.wait_send()


def body(incident, leaf_inverse, contrast, skel_index, ranks, top_core):
    _, fields, leafs = incident.shape
    rows = leaf_inverse.shape[2]
    kmax = skel_index.shape[2]
    boxes, kq = ranks.shape[0], top_core.shape[2]
    chunks = len(CHUNKS)
    wide = 2 * kmax
    dma = pltpu.SemaphoreType.DMA
    vmem = pl.BlockSpec(memory_space=pltpu.VMEM)
    hbm = pl.BlockSpec(memory_space=pltpu.HBM)
    made = [
        ((2, fields, leafs), F32),
        ((2, fields, wide), F32),
        ((2, fields, leafs), BF16),
        ((4, 2, rows, leafs), BF16),
        ((4, 2 * rows, wide), BF16),
        ((kmax, leafs + kmax), BF16),
        ((kmax, leafs + kmax), BF16),
        ((wide, wide), BF16),
        ((wide, wide), BF16),
        ((wide, wide), BF16),
        ((wide, wide), BF16),
        ((8, wide), F32),
    ]

    def in_hbm(value):
        return pltpu.with_memory_space_constraint(value, pltpu.HBM)

    state = pl.pallas_call(
        gather_kernel,
        out_shape=[jax.ShapeDtypeStruct(*each) for each in made],
        in_specs=[hbm] * 5,
        out_specs=[vmem] * len(made),
        scratch_shapes=[
            pltpu.VMEM((3, 2, kmax), jnp.int32),
            pltpu.VMEM((2, boxes), jnp.int32),
            pltpu.VMEM((1, leafs), F32),
            dma((7,)), dma((6,)), dma((6,)),
        ],
        compiler_params=pltpu.CompilerParams(
            collective_id=0, has_side_effects=True, vmem_limit_bytes=24 << 20
        ),
        name="gather",
    )(*map(in_hbm, (incident, leaf_inverse, contrast.reshape(1, leafs), skel_index, ranks.T)))
    return pl.pallas_call(
        merge_kernel,
        out_shape=jax.ShapeDtypeStruct(incident.shape, F32),
        in_specs=[vmem] * len(made) + [hbm],
        out_specs=vmem,
        scratch_shapes=[
            pltpu.VMEM((4, 2, kq, kmax), BF16),
            pltpu.VMEM((wide, wide), BF16),
            pltpu.VMEM((2, fields, wide), BF16),
            pltpu.VMEM((2, fields, wide), BF16),
            pltpu.VMEM((fields, wide), jnp.int16),
            pltpu.VMEM((fields, wide), jnp.int16),
            pltpu.VMEM((chunks, 8, kmax), F32),
            pltpu.VMEM((chunks, 8, kmax), F32),
            pltpu.VMEM((2, fields, kmax), F32),
            pltpu.VMEM((max(CHUNKS), wide), F32),
            dma, dma((3,)), dma((3,)),
            dma((chunks,)), dma((chunks,)), dma((chunks,)), dma((chunks,)),
            dma((chunks,)), dma((chunks,)),
        ],
        compiler_params=pltpu.CompilerParams(
            collective_id=1, has_side_effects=True, vmem_limit_bytes=28 << 20
        ),
        name="merge",
    )(*state, in_hbm(jnp.swapaxes(top_core, 1, 2)))


def solution(mesh):
    return jax.shard_map(
        body,
        mesh=mesh,
        in_specs=(
            P(None, "field", "box"),
            P("box", None, "field", None),
            P("box"),
            P(),
            P(),
            P(None, None, "box"),
        ),
        out_specs=P(None, "field", "box"),
        check_vma=False,
    )
```

```python
import functools

import jax
import jax.numpy as jnp
from jax import lax
from jax.experimental import pallas as pl
from jax.experimental.pallas import tpu as pltpu
from jax.sharding import PartitionSpec as P

MESH = pl.DeviceIdType.MESH
WAVENUM = 0.7
F32 = jnp.float32
BF16 = jnp.bfloat16
CHUNKS = (64, 160, 160, 128)
TOP = 32767.0


def dot_nn(lhs, rhs):
    return lax.dot_general(lhs, rhs, (((1,), (0,)), ((), ())), preferred_element_type=F32)


def dot_nt(lhs, rhs):
    return lax.dot_general(lhs, rhs, (((1,), (1,)), ((), ())), preferred_element_type=F32)


def halves(value):
    high = value.astype(BF16)
    low = (value - high.astype(F32)).astype(BF16)
    return high, low


def grid_of(index):
    return tuple(part.astype(F32) for part in (index & 7, (index >> 3) & 7, index >> 6))


def green(far_col, own_row, apart):
    fx, fy, fz = grid_of(far_col)
    ox, oy, oz = grid_of(own_row)
    dx = fx - (ox - apart)
    dy = fy - oy
    dz = fz - oz
    square = dx * dx + dy * dy + dz * dz
    inverse = lax.rsqrt(square)
    inverse = inverse * (1.5 - 0.5 * square * inverse * inverse)
    turn = WAVENUM * (square * inverse)
    quarter = jnp.floor(turn * 0.6366197723675814 + 0.5)
    rest = (turn - quarter * 1.5703125) - quarter * 4.838267948966e-4
    sq = rest * rest
    sine = rest + rest * sq * (
        -1.6666654611e-1 + sq * (8.3321608736e-3 - sq * 1.9515295891e-4)
    )
    cosine = 1.0 + sq * (
        -0.5 + sq * (4.166664568298827e-2 + sq * (-1.388731625493765e-3 + sq * 2.443315711809948e-5))
    )
    turns = quarter.astype(jnp.int32)
    odd = (turns & 1) == 1
    minus = -inverse
    re = jnp.where(odd, sine, cosine) * jnp.where(((turns + 1) & 2) == 0, inverse, minus)
    im = jnp.where(odd, cosine, sine) * jnp.where((turns & 2) == 0, inverse, minus)
    return re, im


def put_complex(ref, re, im):
    half = re.shape[0]
    ref[:half, :half] = re
    ref[:half, half:] = im
    ref[half:, :half] = -im
    ref[half:, half:] = re


def remote(src, dst, send, recv, peer):
    copy = pltpu.make_async_remote_copy(
        src_ref=src, dst_ref=dst, send_sem=send, recv_sem=recv,
        device_id=peer, device_id_type=MESH,
    )
    copy.start()
    return copy


def meet(peers):
    barrier = pltpu.get_barrier_semaphore()
    for peer in peers:
        pl.semaphore_signal(barrier, inc=1, device_id=peer, device_id_type=MESH)
    return barrier


def places():
    box = lax.axis_index("box")
    me = lax.axis_index("field")
    box1 = box + 1 - 2 * (box % 2)
    box2 = box + 2 - 4 * ((box // 2) % 2)
    return box, me, box1, box2, box2 + 1 - 2 * (box % 2)


def leaf_part(x, matrix, picks, at_f):
    rows = matrix.shape[0] // 2
    by_re = dot_nt(x[0, at_f, :], matrix)
    by_im = dot_nt(x[1, at_f, :], matrix)
    y_re = by_re[:, :rows] - by_im[:, rows:]
    y_im = by_re[:, rows:] + by_im[:, :rows]
    high, low = halves(jnp.concatenate([y_re, y_im], axis=0))
    return y_re, y_im, dot_nn(jnp.concatenate([high, low], axis=1), picks)


def coupled(high, low, ref_h, ref_l):
    size = high.shape[0]
    main = dot_nn(jnp.concatenate([high, low], axis=0), ref_h[...])
    return main[:size] + main[size:] + dot_nn(high, ref_l[...])


def spread(value, matrix):
    kmax = matrix.shape[0]
    size = 2 * value.shape[0]
    high, low = halves(jnp.concatenate([value[:, :kmax], value[:, kmax:]], axis=0))
    parts = dot_nn(jnp.concatenate([high, low], axis=0), matrix)
    return parts[:size] + parts[size:]


def third_part(c, cr, sr, v, es1, g1h, g1l, cc, held):
    size = CHUNKS[c]
    kmax = es1.shape[0]
    leafs = es1.shape[1] - kmax
    at_f = pl.ds(sum(CHUNKS[:c]), size)
    step = sr[c][0:1]
    step = jnp.concatenate([step, step], axis=1)
    high, low = halves(cr[at_f, :].astype(jnp.int32).astype(F32) * step)
    pushed = coupled(high, low, g1h, g1l)
    held[:size] = pushed
    again = spread(pushed, es1[:, leafs:])
    coarse = jnp.concatenate(
        [v[0, at_f, :] - again[:size], v[1, at_f, :] - again[size:]], axis=1
    )
    high, low = halves(coarse)
    main = dot_nn(jnp.concatenate([high, low], axis=0), cc[...])
    total = held[:size] + (main[:size] + main[size:])
    moved = spread(total, es1[:, :leafs])
    return moved[:size], moved[size:]


def solve_kernel(
    inc, leaf, con, skel, rank_in, core,
    out, cr, sr, v, es1, g1h, g1l, cc,
    x, a, et, es0, g0h, g0l, va, idx, rank, cont, cq, ws, wr, cs, ss, held,
    lsem, xsend, xrecv, csend, crecv, wsend, wrecv, ksend, krecv, ssend, srecv,
):
    fields, leafs = inc.shape[1], inc.shape[2]
    kmax = skel.shape[2]
    rows = leaf.shape[2]
    box, me, box1, box2, box3 = places()
    right, left, across = (me + 1) % 4, (me + 3) % 4, (me + 2) % 4
    quad = box % 4

    def local(src, dst, at):
        copy = pltpu.make_async_copy(src, dst, lsem.at[at])
        copy.start()
        return copy

    barrier = meet(((box, right), (box, left), (box1, me), (box2, me), (box3, me)))
    load_idx = [
        local(skel.at[who], idx.at[at], at) for at, who in enumerate((box, box1, box2))
    ]
    load_rank = local(rank_in, rank, 3)
    load_con = local(con, cont, 4)
    load_x = local(inc, x, 5)
    load_a = local(leaf.at[0], a.at[me], 6)
    load_c = local(core, cq.at[quad], 7)
    pl.semaphore_wait(barrier, 5)

    def ring(src, owner, part, at, to):
        return remote(src, a.at[owner, part], xsend.at[at], xrecv.at[at], (box, to))

    from_left_re = ring(leaf.at[0, 0], me, 0, 0, right)
    from_right_im = ring(leaf.at[0, 1], me, 1, 3, left)
    from_left_im = ring(leaf.at[0, 1], me, 1, 1, right)
    from_right_re = ring(leaf.at[0, 0], me, 0, 4, left)
    cores = [
        remote(core, cq.at[quad], csend.at[at], crecv.at[at], (who, me))
        for at, who in enumerate((box1, box2, box3))
    ]

    for copy in load_idx:
        copy.wait()
    load_rank.wait()
    load_con.wait()
    own = idx[0]
    own0, own1 = own[0:1], own[1:2]
    far0, far1 = idx[1][0:1], idx[2][1:2]
    at_box = lax.broadcasted_iota(jnp.int32, rank.shape, 1) == box
    ranks = jnp.sum(jnp.where(at_box, rank[...].astype(F32), 0.0), axis=1, keepdims=True)
    at_k = lax.broadcasted_iota(jnp.int32, (1, kmax), 1)
    in0 = at_k.astype(F32) < ranks[0:1]
    in1 = at_k.astype(F32) < ranks[1:2]
    pick0 = jnp.where(in0, own0, -1)
    pick1 = jnp.where(in1, own1, -1)
    pick1_too = jnp.where(in1, own1, -2)
    table = jnp.concatenate([pick0, pick1, far0, far1, own0, own0, own0, own0], axis=0)
    columns = jnp.transpose(table.astype(F32)).astype(jnp.int32)

    both = jnp.concatenate([pick0, pick1], axis=1)
    at_n = lax.broadcasted_iota(jnp.int32, (rows, 2 * kmax), 0)
    contrast = cont[...]
    c_high = contrast.astype(BF16).astype(F32)
    c_mid = (contrast - c_high).astype(BF16).astype(F32)
    c_low = contrast - c_high - c_mid
    zero = jnp.zeros((5, leafs), F32)
    c_rows = jnp.concatenate([c_high, c_mid, c_low, zero], axis=0).astype(BF16)
    weight = jnp.zeros((8, 2 * kmax), F32)
    for block in range(leafs // rows):
        hit = jnp.where(at_n + block * rows == both, 1.0, 0.0).astype(BF16)
        et[block, :rows] = hit
        et[block, rows:] = hit
        weight = weight + dot_nn(c_rows[:, block * rows : (block + 1) * rows], hit)
    weight = jnp.sum(weight, axis=0, keepdims=True)
    q0, q1 = weight[:, :kmax], weight[:, kmax:]

    def whole_block(owner, first):
        matrix = a[owner].reshape(2 * rows, leafs)
        size = min(256, fields)
        for start in range(0, fields, size):
            at_f = pl.ds(start, size)
            y_re, y_im, picked = leaf_part(x, matrix, et[owner], at_f)
            at_cols = pl.ds(pl.multiple_of(owner * rows, rows), rows)
            out[0, at_f, at_cols] = y_re
            out[1, at_f, at_cols] = y_im
            if not first:
                picked = picked + jnp.concatenate([va[0, at_f, :], va[1, at_f, :]], axis=0)
            va[0, at_f, :] = picked[:size]
            va[1, at_f, :] = picked[size:]

    load_x.wait()
    load_a.wait()
    whole_block(me, True)

    g_re, g_im = green(columns[:, 2:3], own0, (8 * (box1 - box)).astype(F32))
    re_h, re_l = halves(g_re)
    im_h, im_l = halves(g_im)
    put_complex(g0h, re_h, im_h)
    put_complex(g0l, re_l, im_l)

    from_left_re.wait_recv()
    on_right = ring(a.at[left, 0], left, 0, 2, right)
    from_right_im.wait_recv()
    on_left = ring(a.at[right, 1], right, 1, 5, left)

    at_l = lax.broadcasted_iota(jnp.int32, (1, leafs), 1)
    lanes = jnp.concatenate([at_l, pick1_too], axis=1)
    es0[...] = jnp.where(columns[:, 0:1] == lanes, 1.0, 0.0).astype(BF16)
    es1[...] = jnp.where(columns[:, 1:2] == lanes, 1.0, 0.0).astype(BF16)

    from_left_im.wait_recv()
    whole_block(left, False)
    from_right_re.wait_recv()
    whole_block(right, False)

    g_re, g_im = green(columns[:, 3:4], own1, (8 * (box2 - box)).astype(F32))
    re_h, re_l = halves(g_re)
    im_h, im_l = halves(g_im)
    put_complex(g1h, re_h, im_h)
    put_complex(g1l, re_l, im_l)

    load_c.wait()
    for copy in cores:
        copy.wait_recv()
    c_re = jnp.concatenate([cq[at, 0] for at in range(4)], axis=0)
    c_im = jnp.concatenate([cq[at, 1] for at in range(4)], axis=0)
    put_complex(cc, c_re, c_im)

    on_right.wait_recv()
    on_left.wait_recv()
    starts = [sum(CHUNKS[:c]) for c in range(len(CHUNKS))]

    def first_compute(c):
        size = CHUNKS[c]
        at_f = pl.ds(starts[c], size)
        matrix = a[across].reshape(2 * rows, leafs)
        y_re, y_im, picked = leaf_part(x, matrix, et[across], at_f)
        at_cols = pl.ds(pl.multiple_of(across * rows, rows), rows)
        v_re = va[0, at_f, :] + picked[:size]
        v_im = va[1, at_f, :] + picked[size:]
        v[0, at_f, :] = v_re[:, kmax:]
        v[1, at_f, :] = v_im[:, kmax:]
        value = jnp.concatenate([v_re[:, :kmax] * q0, v_im[:, :kmax] * q0], axis=1)
        ws[0, at_f, :], ws[1, at_f, :] = halves(value)
        out[0, at_f, at_cols] = y_re
        out[1, at_f, at_cols] = y_im

    def first_send(c):
        at_f = pl.ds(starts[c], CHUNKS[c])
        return remote(ws.at[:, at_f], wr.at[:, at_f], wsend.at[c], wrecv.at[c], (box1, me))

    def second_stage(c, arriving):
        size = CHUNKS[c]
        at_f = pl.ds(starts[c], size)
        arriving.wait_recv()
        pushed = coupled(wr[0, at_f, :], wr[1, at_f, :], g0h, g0l)
        moved = spread(pushed, es0[...])
        v_re = v[0, at_f, :] - moved[:size, leafs:]
        v_im = v[1, at_f, :] - moved[size:, leafs:]
        v[0, at_f, :] = v_re
        v[1, at_f, :] = v_im
        most = jnp.max(jnp.maximum(jnp.abs(v_re), jnp.abs(v_im)), axis=0, keepdims=True)
        most = jnp.maximum(most, 1e-30)
        scale = TOP / most
        cs[at_f, :kmax] = jnp.round(v_re * scale).astype(jnp.int32).astype(jnp.int16)
        cs[at_f, kmax:] = jnp.round(v_im * scale).astype(jnp.int32).astype(jnp.int16)
        ss[c] = jnp.broadcast_to(most * (1.0 / TOP) * q1, (8, kmax))
        codes = remote(cs.at[at_f], cr.at[at_f], ksend.at[c], krecv.at[c], (box2, me))
        steps = remote(ss.at[c], sr.at[c], ssend.at[c], srecv.at[c], (box2, me))
        out[0, at_f, :] = out[0, at_f, :] - moved[:size, :leafs]
        out[1, at_f, :] = out[1, at_f, :] - moved[size:, :leafs]
        return codes, steps

    def third_stage(c):
        at_f = pl.ds(starts[c], CHUNKS[c])
        codes[c][0].wait_recv()
        codes[c][1].wait_recv()
        m_re, m_im = third_part(c, cr, sr, v, es1, g1h, g1l, cc, held)
        out[0, at_f, :] = out[0, at_f, :] - m_re
        out[1, at_f, :] = out[1, at_f, :] - m_im

    sent = {}
    codes = {}
    for c, late in ((0, False), (1, False), (0, True), (1, True), (2, False), (3, False), (2, True), (3, True)):
        if late:
            codes[c] = second_stage(c, sent[c])
        else:
            first_compute(c)
            sent[c] = first_send(c)
    last = len(CHUNKS) - 1
    for c in range(last):
        third_stage(c)
    codes[last][0].wait_recv()
    codes[last][1].wait_recv()

    for copy in (from_left_re, from_left_im, from_right_im, from_right_re, on_right, on_left):
        copy.wait_send()
    for copy in cores + list(sent.values()):
        copy.wait_send()
    for pair in codes.values():
        for copy in pair:
            copy.wait_send()


def finish_kernel(y, cr, sr, v, es1, g1h, g1l, cc, out, held, done, sem):
    last = len(CHUNKS) - 1
    start, size = sum(CHUNKS[:last]), CHUNKS[last]
    front, back = pl.ds(0, start), pl.ds(start, size)
    early = pltpu.make_async_copy(y.at[:, front], out.at[:, front], sem.at[0])
    early.start()
    m_re, m_im = third_part(last, cr, sr, v, es1, g1h, g1l, cc, held)
    done[0] = y[0, back, :] - m_re
    done[1] = y[1, back, :] - m_im
    rest = pltpu.make_async_copy(done, out.at[:, back], sem.at[1])
    rest.start()
    early.wait()
    rest.wait()


def body(incident, leaf_inverse, contrast, skel_index, ranks, top_core):
    _, fields, leafs = incident.shape
    rows = leaf_inverse.shape[2]
    kmax = skel_index.shape[2]
    boxes, kq = ranks.shape[0], top_core.shape[2]
    chunks = len(CHUNKS)
    wide = 2 * kmax
    dma = pltpu.SemaphoreType.DMA
    vmem = pl.BlockSpec(memory_space=pltpu.VMEM)
    hbm = pl.BlockSpec(memory_space=pltpu.HBM)
    made = [
        ((2, fields, leafs), F32),
        ((fields, wide), jnp.int16),
        ((chunks, 8, kmax), F32),
        ((2, fields, kmax), F32),
        ((kmax, leafs + kmax), BF16),
        ((wide, wide), BF16),
        ((wide, wide), BF16),
        ((wide, wide), BF16),
    ]
    operands = (
        incident,
        leaf_inverse,
        contrast.reshape(1, leafs),
        skel_index,
        ranks.T,
        jnp.swapaxes(top_core, 1, 2),
    )
    state = pl.pallas_call(
        solve_kernel,
        out_shape=[jax.ShapeDtypeStruct(*each) for each in made],
        in_specs=[hbm] * len(operands),
        out_specs=[vmem] * len(made),
        scratch_shapes=[
            pltpu.VMEM((2, fields, leafs), BF16),
            pltpu.VMEM((4, 2, rows, leafs), BF16),
            pltpu.VMEM((4, 2 * rows, wide), BF16),
            pltpu.VMEM((kmax, leafs + kmax), BF16),
            pltpu.VMEM((wide, wide), BF16),
            pltpu.VMEM((wide, wide), BF16),
            pltpu.VMEM((2, fields, wide), F32),
            pltpu.VMEM((3, 2, kmax), jnp.int32),
            pltpu.VMEM((2, boxes), jnp.int32),
            pltpu.VMEM((1, leafs), F32),
            pltpu.VMEM((4, 2, kq, kmax), BF16),
            pltpu.VMEM((2, fields, wide), BF16),
            pltpu.VMEM((2, fields, wide), BF16),
            pltpu.VMEM((fields, wide), jnp.int16),
            pltpu.VMEM((chunks, 8, kmax), F32),
            pltpu.VMEM((max(CHUNKS), wide), F32),
            dma((8,)), dma((6,)), dma((6,)), dma((3,)), dma((3,)),
            dma((chunks,)), dma((chunks,)), dma((chunks,)), dma((chunks,)),
            dma((chunks,)), dma((chunks,)),
        ],
        compiler_params=pltpu.CompilerParams(
            collective_id=0, has_side_effects=True, vmem_limit_bytes=32 << 20
        ),
        name="solve",
    )(*(pltpu.with_memory_space_constraint(value, pltpu.HBM) for value in operands))
    return pl.pallas_call(
        finish_kernel,
        out_shape=jax.ShapeDtypeStruct(incident.shape, F32),
        in_specs=[vmem] * len(made),
        out_specs=hbm,
        scratch_shapes=[
            pltpu.VMEM((CHUNKS[-1], wide), F32),
            pltpu.VMEM((2, CHUNKS[-1], leafs), F32),
            dma((2,)),
        ],
        compiler_params=pltpu.CompilerParams(vmem_limit_bytes=16 << 20),
        name="finish",
    )(*state)


def solution(mesh):
    return jax.shard_map(
        body,
        mesh=mesh,
        in_specs=(
            P(None, "field", "box"),
            P("box", None, "field", None),
            P("box"),
            P(),
            P(),
            P(None, None, "box"),
        ),
        out_specs=P(None, "field", "box"),
        check_vma=False,
    )
```

```python
import functools

import jax
import jax.numpy as jnp
from jax import lax
from jax.experimental import pallas as pl
from jax.experimental.pallas import tpu as pltpu
from jax.sharding import PartitionSpec as P

MESH = pl.DeviceIdType.MESH
WAVENUM = 0.7
F32 = jnp.float32
BF16 = jnp.bfloat16
CHUNKS = (64, 160, 192, 96)
TOP = 32767.0


def dot_nn(lhs, rhs):
    return lax.dot_general(lhs, rhs, (((1,), (0,)), ((), ())), preferred_element_type=F32)


def dot_nt(lhs, rhs):
    return lax.dot_general(lhs, rhs, (((1,), (1,)), ((), ())), preferred_element_type=F32)


def halves(value):
    high = value.astype(BF16)
    low = (value - high.astype(F32)).astype(BF16)
    return high, low


def grid_of(index):
    return tuple(part.astype(F32) for part in (index & 7, (index >> 3) & 7, index >> 6))


def green(far_col, own_row, apart):
    fx, fy, fz = grid_of(far_col)
    ox, oy, oz = grid_of(own_row)
    dx = fx - (ox - apart)
    dy = fy - oy
    dz = fz - oz
    square = dx * dx + dy * dy + dz * dz
    inverse = lax.rsqrt(square)
    inverse = inverse * (1.5 - 0.5 * square * inverse * inverse)
    turn = WAVENUM * (square * inverse)
    quarter = jnp.floor(turn * 0.6366197723675814 + 0.5)
    rest = (turn - quarter * 1.5703125) - quarter * 4.838267948966e-4
    sq = rest * rest
    sine = rest + rest * sq * (
        -1.6666654611e-1 + sq * (8.3321608736e-3 - sq * 1.9515295891e-4)
    )
    cosine = 1.0 + sq * (
        -0.5 + sq * (4.166664568298827e-2 + sq * (-1.388731625493765e-3 + sq * 2.443315711809948e-5))
    )
    turns = quarter.astype(jnp.int32)
    odd = (turns & 1) == 1
    minus = -inverse
    re = jnp.where(odd, sine, cosine) * jnp.where(((turns + 1) & 2) == 0, inverse, minus)
    im = jnp.where(odd, cosine, sine) * jnp.where((turns & 2) == 0, inverse, minus)
    return re, im


def put_complex(ref, re, im):
    half = re.shape[0]
    ref[:half, :half] = re
    ref[:half, half:] = im
    ref[half:, :half] = -im
    ref[half:, half:] = re


def remote(src, dst, send, recv, peer):
    copy = pltpu.make_async_remote_copy(
        src_ref=src, dst_ref=dst, send_sem=send, recv_sem=recv,
        device_id=peer, device_id_type=MESH,
    )
    copy.start()
    return copy


def meet(peers):
    barrier = pltpu.get_barrier_semaphore()
    for peer in peers:
        pl.semaphore_signal(barrier, inc=1, device_id=peer, device_id_type=MESH)
    return barrier


def places():
    box = lax.axis_index("box")
    me = lax.axis_index("field")
    box1 = box + 1 - 2 * (box % 2)
    box2 = box + 2 - 4 * ((box // 2) % 2)
    return box, me, box1, box2, box2 + 1 - 2 * (box % 2)


def leaf_part(x, matrix, picks, at_f):
    rows = matrix.shape[0] // 2
    by_re = dot_nt(x[0, at_f, :], matrix)
    by_im = dot_nt(x[1, at_f, :], matrix)
    y_re = by_re[:, :rows] - by_im[:, rows:]
    y_im = by_re[:, rows:] + by_im[:, :rows]
    high, low = halves(jnp.concatenate([y_re, y_im], axis=0))
    return y_re, y_im, dot_nn(jnp.concatenate([high, low], axis=1), picks)


def coupled(high, low, ref_h, ref_l):
    size = high.shape[0]
    main = dot_nn(jnp.concatenate([high, low], axis=0), ref_h[...])
    return main[:size] + main[size:] + dot_nn(high, ref_l[...])


def spread(value, matrix):
    kmax = matrix.shape[0]
    size = 2 * value.shape[0]
    high, low = halves(jnp.concatenate([value[:, :kmax], value[:, kmax:]], axis=0))
    parts = dot_nn(jnp.concatenate([high, low], axis=0), matrix)
    return parts[:size] + parts[size:]


def third_part(c, cr, sr, v, es1, g1h, g1l, cc, held):
    size = CHUNKS[c]
    kmax = es1.shape[0]
    leafs = es1.shape[1] - kmax
    at_f = pl.ds(sum(CHUNKS[:c]), size)
    step = sr[c][0:1]
    step = jnp.concatenate([step, step], axis=1)
    high, low = halves(cr[at_f, :].astype(jnp.int32).astype(F32) * step)
    pushed = coupled(high, low, g1h, g1l)
    held[:size] = pushed
    again = spread(pushed, es1[:, leafs:])
    coarse = jnp.concatenate(
        [v[0, at_f, :] - again[:size], v[1, at_f, :] - again[size:]], axis=1
    )
    high, low = halves(coarse)
    main = dot_nn(jnp.concatenate([high, low], axis=0), cc[...])
    total = held[:size] + (main[:size] + main[size:])
    moved = spread(total, es1[:, :leafs])
    return moved[:size], moved[size:]


def solve_kernel(
    inc, leaf, con, skel, rank_in, core,
    out, cr, sr, v, es1, g1h, g1l, cc,
    x, a, et, es0, g0h, g0l, va, idx, rank, cont, cq, ws, wr, cs, ss, held,
    lsem, xsend, xrecv, csend, crecv, wsend, wrecv, ksend, krecv, ssend, srecv,
):
    fields, leafs = inc.shape[1], inc.shape[2]
    kmax = skel.shape[2]
    rows = leaf.shape[2]
    box, me, box1, box2, box3 = places()
    right, left, across = (me + 1) % 4, (me + 3) % 4, (me + 2) % 4
    quad = box % 4

    def local(src, dst, at):
        copy = pltpu.make_async_copy(src, dst, lsem.at[at])
        copy.start()
        return copy

    barrier = meet(((box, right), (box, left), (box1, me), (box2, me), (box3, me)))
    load_idx = [
        local(skel.at[who], idx.at[at], at) for at, who in enumerate((box, box1, box2))
    ]
    load_rank = local(rank_in, rank, 3)
    load_con = local(con, cont, 4)
    load_x = local(inc, x, 5)
    load_a = local(leaf.at[0], a.at[me], 6)
    load_c = local(core, cq.at[quad], 7)
    pl.semaphore_wait(barrier, 5)

    def ring(src, owner, part, at, to):
        return remote(src, a.at[owner, part], xsend.at[at], xrecv.at[at], (box, to))

    from_left_re = ring(leaf.at[0, 0], me, 0, 0, right)
    from_right_im = ring(leaf.at[0, 1], me, 1, 3, left)
    from_left_im = ring(leaf.at[0, 1], me, 1, 1, right)
    from_right_re = ring(leaf.at[0, 0], me, 0, 4, left)
    cores = [
        remote(core, cq.at[quad], csend.at[at], crecv.at[at], (who, me))
        for at, who in enumerate((box1, box2, box3))
    ]

    for copy in load_idx:
        copy.wait()
    load_rank.wait()
    load_con.wait()
    own = idx[0]
    own0, own1 = own[0:1], own[1:2]
    far0, far1 = idx[1][0:1], idx[2][1:2]
    at_box = lax.broadcasted_iota(jnp.int32, rank.shape, 1) == box
    ranks = jnp.sum(jnp.where(at_box, rank[...].astype(F32), 0.0), axis=1, keepdims=True)
    at_k = lax.broadcasted_iota(jnp.int32, (1, kmax), 1)
    in0 = at_k.astype(F32) < ranks[0:1]
    in1 = at_k.astype(F32) < ranks[1:2]
    pick0 = jnp.where(in0, own0, -1)
    pick1 = jnp.where(in1, own1, -1)
    pick1_too = jnp.where(in1, own1, -2)
    table = jnp.concatenate([pick0, pick1, far0, far1, own0, own0, own0, own0], axis=0)
    columns = jnp.transpose(table.astype(F32)).astype(jnp.int32)

    both = jnp.concatenate([pick0, pick1], axis=1)
    at_n = lax.broadcasted_iota(jnp.int32, (rows, 2 * kmax), 0)
    contrast = cont[...]
    c_high = contrast.astype(BF16).astype(F32)
    c_mid = (contrast - c_high).astype(BF16).astype(F32)
    c_low = contrast - c_high - c_mid
    zero = jnp.zeros((5, leafs), F32)
    c_rows = jnp.concatenate([c_high, c_mid, c_low, zero], axis=0).astype(BF16)
    weight = jnp.zeros((8, 2 * kmax), F32)
    for block in range(leafs // rows):
        hit = jnp.where(at_n + block * rows == both, 1.0, 0.0).astype(BF16)
        et[block, :rows] = hit
        et[block, rows:] = hit
        weight = weight + dot_nn(c_rows[:, block * rows : (block + 1) * rows], hit)
    weight = jnp.sum(weight, axis=0, keepdims=True)
    q0, q1 = weight[:, :kmax], weight[:, kmax:]

    def whole_block(owner, first):
        matrix = a[owner].reshape(2 * rows, leafs)
        size = min(256, fields)
        for start in range(0, fields, size):
            at_f = pl.ds(start, size)
            y_re, y_im, picked = leaf_part(x, matrix, et[owner], at_f)
            at_cols = pl.ds(pl.multiple_of(owner * rows, rows), rows)
            out[0, at_f, at_cols] = y_re
            out[1, at_f, at_cols] = y_im
            if not first:
                picked = picked + jnp.concatenate([va[0, at_f, :], va[1, at_f, :]], axis=0)
            va[0, at_f, :] = picked[:size]
            va[1, at_f, :] = picked[size:]

    load_x.wait()
    load_a.wait()
    whole_block(me, True)

    from_left_re.wait_recv()
    on_right = ring(a.at[left, 0], left, 0, 2, right)
    from_right_im.wait_recv()
    on_left = ring(a.at[right, 1], right, 1, 5, left)

    g_re, g_im = green(columns[:, 2:3], own0, (8 * (box1 - box)).astype(F32))
    re_h, re_l = halves(g_re)
    im_h, im_l = halves(g_im)
    put_complex(g0h, re_h, im_h)
    put_complex(g0l, re_l, im_l)

    at_l = lax.broadcasted_iota(jnp.int32, (1, leafs), 1)
    lanes = jnp.concatenate([at_l, pick1_too], axis=1)
    es0[...] = jnp.where(columns[:, 0:1] == lanes, 1.0, 0.0).astype(BF16)
    es1[...] = jnp.where(columns[:, 1:2] == lanes, 1.0, 0.0).astype(BF16)

    from_left_im.wait_recv()
    whole_block(left, False)
    from_right_re.wait_recv()
    whole_block(right, False)

    g_re, g_im = green(columns[:, 3:4], own1, (8 * (box2 - box)).astype(F32))
    re_h, re_l = halves(g_re)
    im_h, im_l = halves(g_im)
    put_complex(g1h, re_h, im_h)
    put_complex(g1l, re_l, im_l)

    load_c.wait()
    for copy in cores:
        copy.wait_recv()
    c_re = jnp.concatenate([cq[at, 0] for at in range(4)], axis=0)
    c_im = jnp.concatenate([cq[at, 1] for at in range(4)], axis=0)
    put_complex(cc, c_re, c_im)

    on_right.wait_recv()
    on_left.wait_recv()
    starts = [sum(CHUNKS[:c]) for c in range(len(CHUNKS))]

    def first_compute(c):
        size = CHUNKS[c]
        at_f = pl.ds(starts[c], size)
        matrix = a[across].reshape(2 * rows, leafs)
        y_re, y_im, picked = leaf_part(x, matrix, et[across], at_f)
        at_cols = pl.ds(pl.multiple_of(across * rows, rows), rows)
        v_re = va[0, at_f, :] + picked[:size]
        v_im = va[1, at_f, :] + picked[size:]
        v[0, at_f, :] = v_re[:, kmax:]
        v[1, at_f, :] = v_im[:, kmax:]
        value = jnp.concatenate([v_re[:, :kmax] * q0, v_im[:, :kmax] * q0], axis=1)
        ws[0, at_f, :], ws[1, at_f, :] = halves(value)
        out[0, at_f, at_cols] = y_re
        out[1, at_f, at_cols] = y_im

    def first_send(c):
        at_f = pl.ds(starts[c], CHUNKS[c])
        return remote(ws.at[:, at_f], wr.at[:, at_f], wsend.at[c], wrecv.at[c], (box1, me))

    def second_stage(c, arriving):
        size = CHUNKS[c]
        at_f = pl.ds(starts[c], size)
        arriving.wait_recv()
        pushed = coupled(wr[0, at_f, :], wr[1, at_f, :], g0h, g0l)
        high, low = halves(jnp.concatenate([pushed[:, :kmax], pushed[:, kmax:]], axis=0))
        stacked = jnp.concatenate([high, low], axis=0)
        parts = dot_nn(stacked, es0[:, leafs:])
        moved = parts[: 2 * size] + parts[2 * size :]
        v_re = v[0, at_f, :] - moved[:size]
        v_im = v[1, at_f, :] - moved[size:]
        v[0, at_f, :] = v_re
        v[1, at_f, :] = v_im
        most = jnp.max(jnp.maximum(jnp.abs(v_re), jnp.abs(v_im)), axis=0, keepdims=True)
        most = jnp.maximum(most, 1e-30)
        scale = TOP / most
        cs[at_f, :kmax] = jnp.round(v_re * scale).astype(jnp.int32).astype(jnp.int16)
        cs[at_f, kmax:] = jnp.round(v_im * scale).astype(jnp.int32).astype(jnp.int16)
        ss[c] = jnp.broadcast_to(most * (1.0 / TOP) * q1, (8, kmax))
        codes = remote(cs.at[at_f], cr.at[at_f], ksend.at[c], krecv.at[c], (box2, me))
        steps = remote(ss.at[c], sr.at[c], ssend.at[c], srecv.at[c], (box2, me))
        parts = dot_nn(stacked, es0[:, :leafs])
        moved = parts[: 2 * size] + parts[2 * size :]
        out[0, at_f, :] = out[0, at_f, :] - moved[:size]
        out[1, at_f, :] = out[1, at_f, :] - moved[size:]
        return codes, steps

    def third_stage(c):
        at_f = pl.ds(starts[c], CHUNKS[c])
        codes[c][0].wait_recv()
        codes[c][1].wait_recv()
        m_re, m_im = third_part(c, cr, sr, v, es1, g1h, g1l, cc, held)
        out[0, at_f, :] = out[0, at_f, :] - m_re
        out[1, at_f, :] = out[1, at_f, :] - m_im

    sent = {}
    codes = {}
    for c, late in ((0, False), (1, False), (0, True), (1, True), (2, False), (3, False), (2, True), (3, True)):
        if late:
            codes[c] = second_stage(c, sent[c])
        else:
            first_compute(c)
            sent[c] = first_send(c)
    last = len(CHUNKS) - 1
    for c in range(last):
        third_stage(c)
    codes[last][0].wait_recv()
    codes[last][1].wait_recv()

    for copy in (from_left_re, from_left_im, from_right_im, from_right_re, on_right, on_left):
        copy.wait_send()
    for copy in cores + list(sent.values()):
        copy.wait_send()
    for pair in codes.values():
        for copy in pair:
            copy.wait_send()


def finish_kernel(y, cr, sr, v, es1, g1h, g1l, cc, out, held, done, sem):
    last = len(CHUNKS) - 1
    start, size = sum(CHUNKS[:last]), CHUNKS[last]
    front, back = pl.ds(0, start), pl.ds(start, size)
    early = pltpu.make_async_copy(y.at[:, front], out.at[:, front], sem.at[0])
    early.start()
    m_re, m_im = third_part(last, cr, sr, v, es1, g1h, g1l, cc, held)
    done[0] = y[0, back, :] - m_re
    done[1] = y[1, back, :] - m_im
    rest = pltpu.make_async_copy(done, out.at[:, back], sem.at[1])
    rest.start()
    early.wait()
    rest.wait()


def body(incident, leaf_inverse, contrast, skel_index, ranks, top_core):
    _, fields, leafs = incident.shape
    rows = leaf_inverse.shape[2]
    kmax = skel_index.shape[2]
    boxes, kq = ranks.shape[0], top_core.shape[2]
    chunks = len(CHUNKS)
    wide = 2 * kmax
    dma = pltpu.SemaphoreType.DMA
    vmem = pl.BlockSpec(memory_space=pltpu.VMEM)
    hbm = pl.BlockSpec(memory_space=pltpu.HBM)
    made = [
        ((2, fields, leafs), F32),
        ((fields, wide), jnp.int16),
        ((chunks, 8, kmax), F32),
        ((2, fields, kmax), F32),
        ((kmax, leafs + kmax), BF16),
        ((wide, wide), BF16),
        ((wide, wide), BF16),
        ((wide, wide), BF16),
    ]
    operands = (
        incident,
        leaf_inverse,
        contrast.reshape(1, leafs),
        skel_index,
        ranks.T,
        jnp.swapaxes(top_core, 1, 2),
    )
    state = pl.pallas_call(
        solve_kernel,
        out_shape=[jax.ShapeDtypeStruct(*each) for each in made],
        in_specs=[hbm] * len(operands),
        out_specs=[vmem] * len(made),
        scratch_shapes=[
            pltpu.VMEM((2, fields, leafs), BF16),
            pltpu.VMEM((4, 2, rows, leafs), BF16),
            pltpu.VMEM((4, 2 * rows, wide), BF16),
            pltpu.VMEM((kmax, leafs + kmax), BF16),
            pltpu.VMEM((wide, wide), BF16),
            pltpu.VMEM((wide, wide), BF16),
            pltpu.VMEM((2, fields, wide), F32),
            pltpu.VMEM((3, 2, kmax), jnp.int32),
            pltpu.VMEM((2, boxes), jnp.int32),
            pltpu.VMEM((1, leafs), F32),
            pltpu.VMEM((4, 2, kq, kmax), BF16),
            pltpu.VMEM((2, fields, wide), BF16),
            pltpu.VMEM((2, fields, wide), BF16),
            pltpu.VMEM((fields, wide), jnp.int16),
            pltpu.VMEM((chunks, 8, kmax), F32),
            pltpu.VMEM((max(CHUNKS), wide), F32),
            dma((8,)), dma((6,)), dma((6,)), dma((3,)), dma((3,)),
            dma((chunks,)), dma((chunks,)), dma((chunks,)), dma((chunks,)),
            dma((chunks,)), dma((chunks,)),
        ],
        compiler_params=pltpu.CompilerParams(
            collective_id=0, has_side_effects=True, vmem_limit_bytes=32 << 20
        ),
        name="solve",
    )(*(pltpu.with_memory_space_constraint(value, pltpu.HBM) for value in operands))
    return pl.pallas_call(
        finish_kernel,
        out_shape=jax.ShapeDtypeStruct(incident.shape, F32),
        in_specs=[vmem] * len(made),
        out_specs=hbm,
        scratch_shapes=[
            pltpu.VMEM((CHUNKS[-1], wide), F32),
            pltpu.VMEM((2, CHUNKS[-1], leafs), F32),
            dma((2,)),
        ],
        compiler_params=pltpu.CompilerParams(vmem_limit_bytes=16 << 20),
        name="finish",
    )(*state)


def solution(mesh):
    return jax.shard_map(
        body,
        mesh=mesh,
        in_specs=(
            P(None, "field", "box"),
            P("box", None, "field", None),
            P("box"),
            P(),
            P(),
            P(None, None, "box"),
        ),
        out_specs=P(None, "field", "box"),
        check_vma=False,
    )
```

```python
import functools

import jax
import jax.numpy as jnp
from jax import lax
from jax.experimental import pallas as pl
from jax.experimental.pallas import tpu as pltpu
from jax.sharding import PartitionSpec as P

MESH = pl.DeviceIdType.MESH
WAVENUM = 0.7
F32 = jnp.float32
BF16 = jnp.bfloat16
CHUNKS = (64, 160, 192, 96)
TOP = 32767.0


def dot_nn(lhs, rhs):
    return lax.dot_general(lhs, rhs, (((1,), (0,)), ((), ())), preferred_element_type=F32)


def dot_nt(lhs, rhs):
    return lax.dot_general(lhs, rhs, (((1,), (1,)), ((), ())), preferred_element_type=F32)


def halves(value):
    high = value.astype(BF16)
    low = (value - high.astype(F32)).astype(BF16)
    return high, low


def grid_of(index):
    return tuple(part.astype(F32) for part in (index & 7, (index >> 3) & 7, index >> 6))


def green(far_col, own_row, apart):
    fx, fy, fz = grid_of(far_col)
    ox, oy, oz = grid_of(own_row)
    dx = fx - (ox - apart)
    dy = fy - oy
    dz = fz - oz
    square = dx * dx + dy * dy + dz * dz
    inverse = lax.rsqrt(square)
    inverse = inverse * (1.5 - 0.5 * square * inverse * inverse)
    turn = WAVENUM * (square * inverse)
    quarter = jnp.floor(turn * 0.6366197723675814 + 0.5)
    rest = (turn - quarter * 1.5703125) - quarter * 4.838267948966e-4
    sq = rest * rest
    sine = rest + rest * sq * (
        -1.6666654611e-1 + sq * (8.3321608736e-3 - sq * 1.9515295891e-4)
    )
    cosine = 1.0 + sq * (
        -0.5 + sq * (4.166664568298827e-2 + sq * (-1.388731625493765e-3 + sq * 2.443315711809948e-5))
    )
    turns = quarter.astype(jnp.int32)
    odd = (turns & 1) == 1
    minus = -inverse
    re = jnp.where(odd, sine, cosine) * jnp.where(((turns + 1) & 2) == 0, inverse, minus)
    im = jnp.where(odd, cosine, sine) * jnp.where((turns & 2) == 0, inverse, minus)
    return re, im


def put_complex(ref, re, im):
    half = re.shape[0]
    ref[:half, :half] = re
    ref[:half, half:] = im
    ref[half:, :half] = -im
    ref[half:, half:] = re


def remote(src, dst, send, recv, peer):
    copy = pltpu.make_async_remote_copy(
        src_ref=src, dst_ref=dst, send_sem=send, recv_sem=recv,
        device_id=peer, device_id_type=MESH,
    )
    copy.start()
    return copy


def meet(peers):
    barrier = pltpu.get_barrier_semaphore()
    for peer in peers:
        pl.semaphore_signal(barrier, inc=1, device_id=peer, device_id_type=MESH)
    return barrier


def places():
    box = lax.axis_index("box")
    me = lax.axis_index("field")
    box1 = box + 1 - 2 * (box % 2)
    box2 = box + 2 - 4 * ((box // 2) % 2)
    return box, me, box1, box2, box2 + 1 - 2 * (box % 2)


def leaf_part(x, matrix, picks, at_f):
    rows = matrix.shape[0] // 2
    by_re = dot_nt(x[0, at_f, :], matrix)
    by_im = dot_nt(x[1, at_f, :], matrix)
    y_re = by_re[:, :rows] - by_im[:, rows:]
    y_im = by_re[:, rows:] + by_im[:, :rows]
    high, low = halves(jnp.concatenate([y_re, y_im], axis=0))
    return y_re, y_im, dot_nn(jnp.concatenate([high, low], axis=1), picks)


def coupled(high, low, ref_h, ref_l):
    size = high.shape[0]
    main = dot_nn(jnp.concatenate([high, low], axis=0), ref_h[...])
    return main[:size] + main[size:] + dot_nn(high, ref_l[...])


def spread(value, matrix):
    kmax = matrix.shape[0]
    size = 2 * value.shape[0]
    high, low = halves(jnp.concatenate([value[:, :kmax], value[:, kmax:]], axis=0))
    parts = dot_nn(jnp.concatenate([high, low], axis=0), matrix)
    return parts[:size] + parts[size:]


def third_part(c, cr, sr, v, es1, g1h, g1l, cc, held):
    size = CHUNKS[c]
    kmax = es1.shape[0]
    leafs = es1.shape[1] - kmax
    at_f = pl.ds(sum(CHUNKS[:c]), size)
    step = sr[c][0:1]
    step = jnp.concatenate([step, step], axis=1)
    high, low = halves(cr[at_f, :].astype(jnp.int32).astype(F32) * step)
    pushed = coupled(high, low, g1h, g1l)
    held[:size] = pushed
    again = spread(pushed, es1[:, leafs:])
    coarse = jnp.concatenate(
        [v[0, at_f, :] - again[:size], v[1, at_f, :] - again[size:]], axis=1
    )
    high, low = halves(coarse)
    main = dot_nn(jnp.concatenate([high, low], axis=0), cc[...])
    total = held[:size] + (main[:size] + main[size:])
    moved = spread(total, es1[:, :leafs])
    return moved[:size], moved[size:]


def solve_kernel(
    inc, leaf, con, skel, rank_in, core,
    out, cr, sr, v, es1, g1h, g1l, cc,
    x, a, et, es0, g0h, g0l, va, idx, rank, cont, cq, ws, wr, cs, ss, held,
    lsem, xsend, xrecv, csend, crecv, wsend, wrecv, ksend, krecv, ssend, srecv,
):
    fields, leafs = inc.shape[1], inc.shape[2]
    kmax = skel.shape[2]
    rows = leaf.shape[2]
    box, me, box1, box2, box3 = places()
    right, left, across = (me + 1) % 4, (me + 3) % 4, (me + 2) % 4
    quad = box % 4

    def local(src, dst, at):
        copy = pltpu.make_async_copy(src, dst, lsem.at[at])
        copy.start()
        return copy

    barrier = meet(((box, right), (box, left), (box1, me), (box2, me), (box3, me)))
    load_idx = [
        local(skel.at[who], idx.at[at], at) for at, who in enumerate((box, box1, box2))
    ]
    load_rank = local(rank_in, rank, 3)
    load_con = local(con, cont, 4)
    load_x = local(inc, x, 5)
    load_a = local(leaf.at[0], a.at[me], 6)
    load_c = local(core, cq.at[quad], 7)
    pl.semaphore_wait(barrier, 5)

    def ring(src, owner, part, at, to):
        return remote(src, a.at[owner, part], xsend.at[at], xrecv.at[at], (box, to))

    from_left_re = ring(leaf.at[0, 0], me, 0, 0, right)
    from_right_im = ring(leaf.at[0, 1], me, 1, 3, left)
    from_left_im = ring(leaf.at[0, 1], me, 1, 1, right)
    from_right_re = ring(leaf.at[0, 0], me, 0, 4, left)
    cores = [
        remote(core, cq.at[quad], csend.at[at], crecv.at[at], (who, me))
        for at, who in enumerate((box1, box2, box3))
    ]

    for copy in load_idx:
        copy.wait()
    load_rank.wait()
    load_con.wait()
    own = idx[0]
    own0, own1 = own[0:1], own[1:2]
    far0, far1 = idx[1][0:1], idx[2][1:2]
    at_box = lax.broadcasted_iota(jnp.int32, rank.shape, 1) == box
    ranks = jnp.sum(jnp.where(at_box, rank[...].astype(F32), 0.0), axis=1, keepdims=True)
    at_k = lax.broadcasted_iota(jnp.int32, (1, kmax), 1)
    in0 = at_k.astype(F32) < ranks[0:1]
    in1 = at_k.astype(F32) < ranks[1:2]
    pick0 = jnp.where(in0, own0, -1)
    pick1 = jnp.where(in1, own1, -1)
    pick1_too = jnp.where(in1, own1, -2)
    table = jnp.concatenate([pick0, pick1, far0, far1, own0, own0, own0, own0], axis=0)
    columns = jnp.transpose(table.astype(F32)).astype(jnp.int32)

    both = jnp.concatenate([pick0, pick1], axis=1)
    at_n = lax.broadcasted_iota(jnp.int32, (rows, 2 * kmax), 0)
    contrast = cont[...]
    c_high = contrast.astype(BF16).astype(F32)
    c_mid = (contrast - c_high).astype(BF16).astype(F32)
    c_low = contrast - c_high - c_mid
    zero = jnp.zeros((5, leafs), F32)
    c_rows = jnp.concatenate([c_high, c_mid, c_low, zero], axis=0).astype(BF16)
    weight = jnp.zeros((8, 2 * kmax), F32)
    for block in range(leafs // rows):
        hit = jnp.where(at_n + block * rows == both, 1.0, 0.0).astype(BF16)
        et[block, :rows] = hit
        et[block, rows:] = hit
        weight = weight + dot_nn(c_rows[:, block * rows : (block + 1) * rows], hit)
    weight = jnp.sum(weight, axis=0, keepdims=True)
    q0, q1 = weight[:, :kmax], weight[:, kmax:]

    def whole_block(owner, first):
        matrix = a[owner].reshape(2 * rows, leafs)
        size = min(256, fields)
        for start in range(0, fields, size):
            at_f = pl.ds(start, size)
            y_re, y_im, picked = leaf_part(x, matrix, et[owner], at_f)
            at_cols = pl.ds(pl.multiple_of(owner * rows, rows), rows)
            out[0, at_f, at_cols] = y_re
            out[1, at_f, at_cols] = y_im
            if not first:
                picked = picked + jnp.concatenate([va[0, at_f, :], va[1, at_f, :]], axis=0)
            va[0, at_f, :] = picked[:size]
            va[1, at_f, :] = picked[size:]

    load_x.wait()
    load_a.wait()
    whole_block(me, True)

    g_re, g_im = green(columns[:, 2:3], own0, (8 * (box1 - box)).astype(F32))
    re_h, re_l = halves(g_re)
    im_h, im_l = halves(g_im)
    put_complex(g0h, re_h, im_h)
    put_complex(g0l, re_l, im_l)

    from_left_re.wait_recv()
    on_right = ring(a.at[left, 0], left, 0, 2, right)
    from_right_im.wait_recv()
    on_left = ring(a.at[right, 1], right, 1, 5, left)

    at_l = lax.broadcasted_iota(jnp.int32, (1, leafs), 1)
    lanes = jnp.concatenate([at_l, pick1_too], axis=1)
    es0[...] = jnp.where(columns[:, 0:1] == lanes, 1.0, 0.0).astype(BF16)
    es1[...] = jnp.where(columns[:, 1:2] == lanes, 1.0, 0.0).astype(BF16)

    from_left_im.wait_recv()
    whole_block(left, False)
    from_right_re.wait_recv()
    whole_block(right, False)

    g_re, g_im = green(columns[:, 3:4], own1, (8 * (box2 - box)).astype(F32))
    re_h, re_l = halves(g_re)
    im_h, im_l = halves(g_im)
    put_complex(g1h, re_h, im_h)
    put_complex(g1l, re_l, im_l)

    load_c.wait()
    for copy in cores:
        copy.wait_recv()
    c_re = jnp.concatenate([cq[at, 0] for at in range(4)], axis=0)
    c_im = jnp.concatenate([cq[at, 1] for at in range(4)], axis=0)
    put_complex(cc, c_re, c_im)

    on_right.wait_recv()
    on_left.wait_recv()
    starts = [sum(CHUNKS[:c]) for c in range(len(CHUNKS))]

    def first_compute(c):
        size = CHUNKS[c]
        at_f = pl.ds(starts[c], size)
        matrix = a[across].reshape(2 * rows, leafs)
        y_re, y_im, picked = leaf_part(x, matrix, et[across], at_f)
        at_cols = pl.ds(pl.multiple_of(across * rows, rows), rows)
        v_re = va[0, at_f, :] + picked[:size]
        v_im = va[1, at_f, :] + picked[size:]
        v[0, at_f, :] = v_re[:, kmax:]
        v[1, at_f, :] = v_im[:, kmax:]
        value = jnp.concatenate([v_re[:, :kmax] * q0, v_im[:, :kmax] * q0], axis=1)
        ws[0, at_f, :], ws[1, at_f, :] = halves(value)
        out[0, at_f, at_cols] = y_re
        out[1, at_f, at_cols] = y_im

    def first_send(c):
        at_f = pl.ds(starts[c], CHUNKS[c])
        return remote(ws.at[:, at_f], wr.at[:, at_f], wsend.at[c], wrecv.at[c], (box1, me))

    def second_stage(c, arriving):
        size = CHUNKS[c]
        at_f = pl.ds(starts[c], size)
        arriving.wait_recv()
        pushed = coupled(wr[0, at_f, :], wr[1, at_f, :], g0h, g0l)
        moved = spread(pushed, es0[...])
        v_re = v[0, at_f, :] - moved[:size, leafs:]
        v_im = v[1, at_f, :] - moved[size:, leafs:]
        v[0, at_f, :] = v_re
        v[1, at_f, :] = v_im
        most = jnp.max(jnp.maximum(jnp.abs(v_re), jnp.abs(v_im)), axis=0, keepdims=True)
        most = jnp.maximum(most, 1e-30)
        scale = TOP / most
        cs[at_f, :kmax] = jnp.round(v_re * scale).astype(jnp.int32).astype(jnp.int16)
        cs[at_f, kmax:] = jnp.round(v_im * scale).astype(jnp.int32).astype(jnp.int16)
        ss[c] = jnp.broadcast_to(most * (1.0 / TOP) * q1, (8, kmax))
        codes = remote(cs.at[at_f], cr.at[at_f], ksend.at[c], krecv.at[c], (box2, me))
        steps = remote(ss.at[c], sr.at[c], ssend.at[c], srecv.at[c], (box2, me))
        out[0, at_f, :] = out[0, at_f, :] - moved[:size, :leafs]
        out[1, at_f, :] = out[1, at_f, :] - moved[size:, :leafs]
        return codes, steps

    def third_stage(c):
        at_f = pl.ds(starts[c], CHUNKS[c])
        codes[c][0].wait_recv()
        codes[c][1].wait_recv()
        m_re, m_im = third_part(c, cr, sr, v, es1, g1h, g1l, cc, held)
        out[0, at_f, :] = out[0, at_f, :] - m_re
        out[1, at_f, :] = out[1, at_f, :] - m_im

    sent = {}
    codes = {}
    for c, late in ((0, False), (1, False), (0, True), (1, True), (2, False), (3, False), (2, True), (3, True)):
        if late:
            codes[c] = second_stage(c, sent[c])
        else:
            first_compute(c)
            sent[c] = first_send(c)
    last = len(CHUNKS) - 1
    for c in range(last):
        third_stage(c)
    codes[last][0].wait_recv()
    codes[last][1].wait_recv()

    for copy in (from_left_re, from_left_im, from_right_im, from_right_re, on_right, on_left):
        copy.wait_send()
    for copy in cores + list(sent.values()):
        copy.wait_send()
    for pair in codes.values():
        for copy in pair:
            copy.wait_send()


def finish_kernel(y, cr, sr, v, es1, g1h, g1l, cc, out, held, done, sem):
    last = len(CHUNKS) - 1
    start, size = sum(CHUNKS[:last]), CHUNKS[last]
    front, back = pl.ds(0, start), pl.ds(start, size)
    early = pltpu.make_async_copy(y.at[:, front], out.at[:, front], sem.at[0])
    early.start()
    m_re, m_im = third_part(last, cr, sr, v, es1, g1h, g1l, cc, held)
    done[0] = y[0, back, :] - m_re
    done[1] = y[1, back, :] - m_im
    rest = pltpu.make_async_copy(done, out.at[:, back], sem.at[1])
    rest.start()
    early.wait()
    rest.wait()


def body(incident, leaf_inverse, contrast, skel_index, ranks, top_core):
    _, fields, leafs = incident.shape
    rows = leaf_inverse.shape[2]
    kmax = skel_index.shape[2]
    boxes, kq = ranks.shape[0], top_core.shape[2]
    chunks = len(CHUNKS)
    wide = 2 * kmax
    dma = pltpu.SemaphoreType.DMA
    vmem = pl.BlockSpec(memory_space=pltpu.VMEM)
    hbm = pl.BlockSpec(memory_space=pltpu.HBM)
    made = [
        ((2, fields, leafs), F32),
        ((fields, wide), jnp.int16),
        ((chunks, 8, kmax), F32),
        ((2, fields, kmax), F32),
        ((kmax, leafs + kmax), BF16),
        ((wide, wide), BF16),
        ((wide, wide), BF16),
        ((wide, wide), BF16),
    ]
    operands = (
        incident,
        leaf_inverse,
        contrast.reshape(1, leafs),
        skel_index,
        ranks.T,
        jnp.swapaxes(top_core, 1, 2),
    )
    state = pl.pallas_call(
        solve_kernel,
        out_shape=[jax.ShapeDtypeStruct(*each) for each in made],
        in_specs=[hbm] * len(operands),
        out_specs=[vmem] * len(made),
        scratch_shapes=[
            pltpu.VMEM((2, fields, leafs), BF16),
            pltpu.VMEM((4, 2, rows, leafs), BF16),
            pltpu.VMEM((4, 2 * rows, wide), BF16),
            pltpu.VMEM((kmax, leafs + kmax), BF16),
            pltpu.VMEM((wide, wide), BF16),
            pltpu.VMEM((wide, wide), BF16),
            pltpu.VMEM((2, fields, wide), F32),
            pltpu.VMEM((3, 2, kmax), jnp.int32),
            pltpu.VMEM((2, boxes), jnp.int32),
            pltpu.VMEM((1, leafs), F32),
            pltpu.VMEM((4, 2, kq, kmax), BF16),
            pltpu.VMEM((2, fields, wide), BF16),
            pltpu.VMEM((2, fields, wide), BF16),
            pltpu.VMEM((fields, wide), jnp.int16),
            pltpu.VMEM((chunks, 8, kmax), F32),
            pltpu.VMEM((max(CHUNKS), wide), F32),
            dma((8,)), dma((6,)), dma((6,)), dma((3,)), dma((3,)),
            dma((chunks,)), dma((chunks,)), dma((chunks,)), dma((chunks,)),
            dma((chunks,)), dma((chunks,)),
        ],
        compiler_params=pltpu.CompilerParams(
            collective_id=0, has_side_effects=True, vmem_limit_bytes=32 << 20
        ),
        name="solve",
    )(*(pltpu.with_memory_space_constraint(value, pltpu.HBM) for value in operands))
    return pl.pallas_call(
        finish_kernel,
        out_shape=jax.ShapeDtypeStruct(incident.shape, F32),
        in_specs=[vmem] * len(made),
        out_specs=hbm,
        scratch_shapes=[
            pltpu.VMEM((CHUNKS[-1], wide), F32),
            pltpu.VMEM((2, CHUNKS[-1], leafs), F32),
            dma((2,)),
        ],
        compiler_params=pltpu.CompilerParams(vmem_limit_bytes=16 << 20),
        name="finish",
    )(*state)


def solution(mesh):
    return jax.shard_map(
        body,
        mesh=mesh,
        in_specs=(
            P(None, "field", "box"),
            P("box", None, "field", None),
            P("box"),
            P(),
            P(),
            P(None, None, "box"),
        ),
        out_specs=P(None, "field", "box"),
        check_vma=False,
    )
```
